512 devices in a mesh: dom: 16 (over x_lo, y, core), space: 32 (over x_hi, z).
Axes of the slice: x: 4 (x_hi: 2, x_lo: 2; x = x_hi * 2 + x_lo), y: 4, z: 16, core: 2. Of those that a mesh axis runs over, the one named last changes fastest.
Arguments:
- orbitals: bfloat16 [16, 2, 128, 16, 8, 128], P('dom', None, 'space'), may hold values from -6 to 6
- initial: bfloat16 [16, 2, 128, 16, 8, 128], P('dom', None, 'space'), may hold values from -4 to 4
- potential: float32 [16, 128, 128], P('dom', 'space'), may hold values from -1 to 1
- external: float32 [16, 128, 128], P('dom', 'space'), may hold values from -1 to 1
- occupation: float32 [128], replicated, may hold values from 0.5 to 2
- coupling: float32 [128, 128], replicated, may hold values from -1.25 to 1.25
- neighbours: int32 [16, 2], replicated, may hold values from 0 to 15, as said below
- offsets: int32 [16, 2], replicated, may hold values from 0 to 12
Outputs:
- evolved: bfloat16 [16, 2, 128, 16, 8, 128], P('dom', None, 'space')
- intersection: float32 [16, 2, 128, 128], P('dom')
- new_potential: float32 [16, 128, 128], P('dom', 'space')
The draws below stay inside these ranges and needn't reach their ends.
Inputs may be any that keep to these rules, and one draw needn't show every extreme that they name: Following upper neighbours visits all 16 domains in one cycle, and the lower neighbour of a domain's upper neighbour is that domain.
All inputs are finite; a program needn't handle non-finite values.
Results may differ from the reference program's by a relative error of at most 0.007.
Values may be sent and summed in bfloat16 or wider, within the bound.
No kernel may reach another device: no remote copies, remote signals or barrier semaphores. Data moves between devices by JAX's collectives and lax.ppermute only.
A program may use at most 64 MiB of HBM per device.

```python
import jax
import jax.numpy as jnp
from jax import lax

NORB = 128
GY = 16
GZ = 8
TAYLOR = 4
STEPS = 2
BUF = 4
NDOM = 16
GX = 128
NCELLS = 16384


def orbital_pair(key):
    shape = (NDOM, 2, GX, GY, GZ, NORB)
    key_base = jax.random.fold_in(key, 101)
    key_noise = jax.random.fold_in(key, 102)
    key_real = jax.random.fold_in(key, 103)
    key_imag = jax.random.fold_in(key, 104)
    key_center = jax.random.fold_in(key, 106)
    base = jax.random.truncated_normal(key_base, -4.0, 4.0, shape, jnp.float32) * 0.7071
    noise = jax.random.truncated_normal(key_noise, -4.0, 4.0, shape, jnp.float32)
    centers = jax.random.uniform(key_center, (NDOM, NORB), jnp.float32, 0.0, 1.0 * GX)
    planes = jnp.arange(GX, dtype=jnp.float32)
    distance = (planes[None, :, None] - centers[:, None, :]) / (0.1 * GX)
    envelope = 0.25 + 1.75 * jnp.exp(-0.5 * distance * distance)
    envelope = envelope.reshape(NDOM, 1, GX, 1, 1, NORB)
    base = jnp.clip(base * envelope, -4.0, 4.0)
    spread = 0.5 / NORB ** 0.5
    mix_real = 0.7 * jnp.eye(NORB, dtype=jnp.float32) + spread * jax.random.normal(key_real, (NDOM, NORB, NORB), jnp.float32)
    mix_imag = spread * jax.random.normal(key_imag, (NDOM, NORB, NORB), jnp.float32)
    form = 'dxyzn,dnm->dxyzm'
    high = lax.Precision.HIGHEST
    part_real = jnp.einsum(form, base[:, 0], mix_real, precision=high) - jnp.einsum(form, base[:, 1], mix_imag, precision=high)
    part_imag = jnp.einsum(form, base[:, 0], mix_imag, precision=high) + jnp.einsum(form, base[:, 1], mix_real, precision=high)
    current = jnp.clip(jnp.stack([part_real, part_imag], axis=1) + 0.5 * noise, -6.0, 6.0)
    return (base, current)


def draw_orbitals(key, part):
    base, current = orbital_pair(key)
    return current.astype(jnp.bfloat16)


def draw_initial(key, part):
    base, current = orbital_pair(key)
    return base.astype(jnp.bfloat16)


def draw_neighbours(key, part):
    order = jax.random.permutation(jax.random.fold_in(key, 7), NDOM).astype(jnp.int32)
    upper = jnp.roll(order, -1)
    lower = jnp.roll(order, 1)
    table = jnp.zeros((NDOM, 2), jnp.int32)
    table = table.at[order, 0].set(lower)
    table = table.at[order, 1].set(upper)
    return table


def plant(array, key, low, top_value):
    place = [jax.random.randint(jax.random.fold_in(key, axis), (), 0, length) for axis, length in enumerate(array.shape)]
    main_axis = array.shape.index(max(array.shape))
    beside = place[:main_axis] + [(place[main_axis] + 1) % array.shape[main_axis]] + place[main_axis + 1:]
    return array.at[tuple(place)].set(low).at[tuple(beside)].set(top_value)


def level_of(key, shape, pieces, low, high):
    def one(dim, shards_of):
        draws = jax.random.uniform(jax.random.fold_in(jax.random.fold_in(key, 6), dim), (shards_of,), jnp.float32, low / len(pieces), high / len(pieces))
        return jnp.repeat(jnp.exp(draws), shape[dim] // shards_of).reshape((-1,) + (1,) * (len(shape) - dim - 1))

    loudness = one(*pieces[0])
    for cut in pieces[1:]:
        loudness = loudness * one(*cut)
    return loudness


def scatter_about(rng, dims, scale, most, held_as=jnp.bfloat16):
    result = scale * jax.random.normal(rng, dims, jnp.float32)
    return jnp.clip(result, min=-most, max=most).astype(held_as)


def setup_inputs(seed: int = 0) -> dict:
    key_list = jax.random.split(jax.random.key(seed), 9)
    return {
        "orbitals": draw_orbitals(jax.random.fold_in(key_list[8], 71), 0),
        "initial": draw_initial(jax.random.fold_in(key_list[8], 71), 0),
        "potential": jnp.clip(jax.random.uniform(key_list[2], (NDOM, GX, GY * GZ), jnp.float32, -1.0, 1.0) * level_of(key_list[2], (NDOM, GX, GY * GZ), ((0, 16), (1, 32)), -0.4, 0.0), -1.0, 1.0),
        "external": jnp.clip(jax.random.uniform(key_list[3], (NDOM, GX, GY * GZ), jnp.float32, -1.0, 1.0) * level_of(key_list[3], (NDOM, GX, GY * GZ), ((0, 16), (1, 32)), -0.4, 0.0), -1.0, 1.0),
        "occupation": jnp.clip(jax.random.uniform(key_list[4], (NORB,), jnp.float32, 0.5, 2.0), 0.5, 2.0),
        "coupling": scatter_about(key_list[5], (NORB, NORB), (10.0 / NORB), 1.25, jnp.float32),
        "neighbours": draw_neighbours(jax.random.fold_in(key_list[8], 71), 0),
        "offsets": plant(jax.random.randint(key_list[7], (NDOM, 2), 0, GY - BUF + 1), jax.random.fold_in(key_list[7], 1), 0, GY - BUF).astype(jnp.int32),
    }


time_step = 0.4
half_step = 0.2
xc_factor = 0.9847450218426965


def laplace(source):
    center = source[:, 1:-1]
    total = source[:, 2:] + source[:, :-2] - 6.0 * center
    padded = jnp.pad(center, ((0, 0), (0, 0), (1, 1), (1, 1), (0, 0)))
    total = total + padded[:, :, 2:, 1:-1] + padded[:, :, :-2, 1:-1]
    total = total + padded[:, :, 1:-1, 2:] + padded[:, :, 1:-1, :-2]
    return total


def phase_turn(field, angle):
    cosv = jnp.cos(angle)[..., None]
    sinv = jnp.sin(angle)[..., None]
    return jnp.stack([cosv * field[0] + sinv * field[1], cosv * field[1] - sinv * field[0]])


def kinetic(field):
    running = field
    taylor_term = lax.optimization_barrier(field.astype(jnp.bfloat16))
    for order in range(1, TAYLOR + 1):
        widened = jnp.pad(taylor_term.astype(jnp.float32), ((0, 0), (1, 1), (0, 0), (0, 0), (0, 0)))
        curvature = laplace(widened)
        factor = time_step / (2.0 * order)
        update = jnp.stack([-factor * curvature[1], factor * curvature[0]])
        running = running + update
        taylor_term = lax.optimization_barrier(update.astype(jnp.bfloat16))
    return running


def reference(orbitals, initial, potential, external, occupation, coupling, neighbours, offsets):
    def evolve(items):
        field_in, start, grid_pot = items
        field = field_in.astype(jnp.float32)
        angle = half_step * grid_pot.reshape(GX, GY, GZ)
        flat_start = start.reshape(-1, NORB)
        start_real = start[0].reshape(-1, NORB)
        start_imag = start[1].reshape(-1, NORB)
        intersection = jnp.zeros((2, NORB, NORB), jnp.float32)
        for section in range(STEPS):
            field = phase_turn(field, angle)
            field = kinetic(field)
            field = phase_turn(field, angle)
            rounded = field.astype(jnp.bfloat16)
            over_real = jnp.dot(flat_start.T, rounded.reshape(-1, NORB), preferred_element_type=jnp.float32)
            over_imag = jnp.dot(start_real.T, rounded[1].reshape(-1, NORB), preferred_element_type=jnp.float32) - jnp.dot(start_imag.T, rounded[0].reshape(-1, NORB), preferred_element_type=jnp.float32)
            intersection = jnp.stack([over_real, over_imag]) * (1.0 / NCELLS)
            mix_real = jnp.dot(coupling, intersection[0], precision=lax.Precision.HIGHEST).astype(jnp.bfloat16)
            mix_imag = jnp.dot(coupling, intersection[1], precision=lax.Precision.HIGHEST).astype(jnp.bfloat16)
            corr_real = jnp.dot(start_real, mix_real, preferred_element_type=jnp.float32) - jnp.dot(start_imag, mix_imag, preferred_element_type=jnp.float32)
            corr_imag = jnp.dot(start_real, mix_imag, preferred_element_type=jnp.float32) + jnp.dot(start_imag, mix_real, preferred_element_type=jnp.float32)
            shape_one = (GX, GY, GZ, NORB)
            field = field + time_step * jnp.stack([corr_imag.reshape(shape_one), -corr_real.reshape(shape_one)])
        density = jnp.sum(field * field * occupation, axis=(0, 4))
        return field, intersection, density

    fields, intersections, densities = lax.map(evolve, (orbitals, initial, potential))
    cut = lambda arr, start: lax.dynamic_slice_in_dim(arr, start, BUF, 1)
    lower_bricks = jax.vmap(cut)(densities[neighbours[:, 0]], offsets[:, 0].astype(jnp.int32))
    upper_bricks = jax.vmap(cut)(densities[neighbours[:, 1]], offsets[:, 1].astype(jnp.int32))
    planes = jnp.arange(BUF).astype(jnp.float32)
    weight_low = ((planes + 1.0) / (BUF + 1.0)).reshape(1, 1, BUF, 1)
    weight_high = ((BUF - planes) / (BUF + 1.0)).reshape(1, 1, BUF, 1)
    low = densities[:, :, :BUF] * weight_low + lower_bricks * (1.0 - weight_low)
    high = densities[:, :, GY - BUF:] * weight_high + upper_bricks * (1.0 - weight_high)
    blended = jnp.concatenate([low, densities[:, :, BUF:GY - BUF], high], axis=2)
    new_grid = external.reshape(NDOM, GX, GY, GZ) - xc_factor * jnp.cbrt(blended + 1e-6)

    def finish(items):
        field, grid_pot = items
        return phase_turn(field, half_step * grid_pot).astype(jnp.bfloat16)

    evolved = lax.map(finish, (fields, new_grid))
    return evolved, intersections, new_grid.reshape(NDOM, GX, GY * GZ)
```

```python
import jax
import jax.numpy as jnp
from jax import lax
from jax.sharding import PartitionSpec as P

TAYLOR = 4
BUF = 4

time_step = 0.4
half_step = 0.2
xc_factor = 0.9847450218426965


def halo(value, axis):
    devices = lax.axis_size(axis)
    up = [(i, i + 1) for i in range(devices - 1)]
    down = [(i + 1, i) for i in range(devices - 1)]
    before = lax.ppermute(value, axis, up)
    after = lax.ppermute(value, axis, down)
    return jnp.concatenate([before, value, after], axis=1)


def laplace(source):
    center = source[:, 1:-1]
    total = source[:, 2:] + source[:, :-2] - 6.0 * center
    padded = jnp.pad(center, ((0, 0), (0, 0), (1, 1), (1, 1), (0, 0)))
    total = total + padded[:, :, 2:, 1:-1] + padded[:, :, :-2, 1:-1]
    total = total + padded[:, :, 1:-1, 2:] + padded[:, :, 1:-1, :-2]
    return total


def phase_turn(field, angle):
    cosv = jnp.cos(angle)[..., None]
    sinv = jnp.sin(angle)[..., None]
    return jnp.stack([cosv * field[0] + sinv * field[1], cosv * field[1] - sinv * field[0]])


def kinetic_body(field, wide, inside):
    slab = field.shape[1]
    running = field
    term = wide
    for order in range(1, TAYLOR + 1):
        curvature = laplace(term.astype(jnp.float32))
        factor = time_step / (2.0 * order)
        keep = inside[order : inside.shape[0] - order].reshape(-1, 1, 1, 1) * factor
        update = jnp.stack([-keep * curvature[1], keep * curvature[0]])
        skip = (update.shape[1] - slab) // 2
        running = running + update[:, skip : skip + slab]
        term = lax.optimization_barrier(update.astype(jnp.bfloat16))
    return running


def contract(left, right):
    return lax.dot_general(
        left, right, (((0,), (0,)), ((), ())), preferred_element_type=jnp.float32
    )


def overlap(start_real, start_imag, rounded):
    orbits = start_real.shape[-1]
    real = rounded[0].reshape(-1, orbits)
    imag = rounded[1].reshape(-1, orbits)
    over_real = contract(start_real, real) + contract(start_imag, imag)
    over_imag = contract(start_real, imag) - contract(start_imag, real)
    return jnp.stack([over_real, over_imag])


def space_sum(partial, axis):
    devices = lax.axis_size(axis)
    parts = lax.all_to_all(partial.astype(jnp.bfloat16), axis, 0, 0, tiled=True)
    rows = partial.shape[0] // devices
    mine = jnp.sum(parts.reshape(devices, rows, -1).astype(jnp.float32), axis=0)
    spread = jnp.broadcast_to(mine.astype(jnp.bfloat16)[None], (devices,) + mine.shape)
    return lax.all_to_all(lax.optimization_barrier(spread), axis, 0, 0, tiled=True)


def high_dot(left, right):
    return jnp.dot(left, right, precision=lax.Precision.HIGHEST)


def half_dot(left, right):
    return jnp.dot(left, right, preferred_element_type=jnp.float32)


def select_owner(stacked, owner, domain_ids):
    picked = (domain_ids == owner).reshape((stacked.shape[0],) + (1,) * (stacked.ndim - 1))
    return jnp.sum(jnp.where(picked, stacked, 0.0), axis=0)


def shards(orbitals, initial, potential, external, occupation, coupling, neighbours, offsets):
    start = initial[0]
    slab, rows_y, cols_z, orbits = start.shape[1:]
    devices = lax.axis_size("space")
    place = lax.axis_index("space")
    angle = half_step * potential[0].reshape(slab, rows_y, cols_z)
    cells_total = slab * devices * rows_y * cols_z
    shape_one = (slab, rows_y, cols_z, orbits)
    start_real = start[0].reshape(-1, orbits)
    start_imag = start[1].reshape(-1, orbits)
    low_in = jnp.full((slab,), jnp.where(place > 0, 1.0, 0.0), jnp.float32)
    high_in = jnp.full((slab,), jnp.where(place < devices - 1, 1.0, 0.0), jnp.float32)
    inside = jnp.concatenate([low_in, jnp.ones((slab,), jnp.float32), high_in])

    turned = phase_turn(orbitals[0].astype(jnp.float32), angle)
    turned_start = phase_turn(start.astype(jnp.float32), angle)
    sent = lax.optimization_barrier(turned.astype(jnp.bfloat16))
    sent_start = lax.optimization_barrier(turned_start.astype(jnp.bfloat16))
    wide = halo(sent, "space")
    wide_start = halo(sent_start, "space")
    first = phase_turn(kinetic_body(turned, wide, inside), angle)
    turned = phase_turn(first, angle)
    sent = lax.optimization_barrier(turned.astype(jnp.bfloat16))
    wide = halo(sent, "space")
    moved = phase_turn(kinetic_body(turned_start, wide_start, inside), angle).astype(jnp.bfloat16)
    moved = lax.optimization_barrier(moved)
    second = phase_turn(kinetic_body(turned, wide, inside), angle)

    partial = jnp.concatenate(
        [
            overlap(start_real, start_imag, first.astype(jnp.bfloat16)),
            overlap(start_real, start_imag, second.astype(jnp.bfloat16)),
            overlap(start_real, start_imag, moved),
        ]
    ) * (1.0 / cells_total)
    summed = space_sum(partial.reshape(-1, orbits), "space").reshape(6, orbits, orbits)
    wide_sum = summed.astype(jnp.float32)
    mix1_real = high_dot(coupling, wide_sum[0]).astype(jnp.bfloat16)
    mix1_imag = high_dot(coupling, wide_sum[1]).astype(jnp.bfloat16)
    gram_real, gram_imag = summed[4], summed[5]
    over_real = wide_sum[2] + time_step * (
        half_dot(gram_real, mix1_imag) + half_dot(gram_imag, mix1_real)
    )
    over_imag = wide_sum[3] - time_step * (
        half_dot(gram_real, mix1_real) - half_dot(gram_imag, mix1_imag)
    )
    intersection = jnp.stack([over_real, over_imag])
    mix2_real = high_dot(coupling, over_real).astype(jnp.bfloat16)
    mix2_imag = high_dot(coupling, over_imag).astype(jnp.bfloat16)
    moved_real = moved[0].reshape(-1, orbits)
    moved_imag = moved[1].reshape(-1, orbits)
    corr_real = (
        half_dot(moved_real, mix1_real)
        - half_dot(moved_imag, mix1_imag)
        + half_dot(start_real, mix2_real)
        - half_dot(start_imag, mix2_imag)
    )
    corr_imag = (
        half_dot(moved_real, mix1_imag)
        + half_dot(moved_imag, mix1_real)
        + half_dot(start_real, mix2_imag)
        + half_dot(start_imag, mix2_real)
    )
    field = second + time_step * jnp.stack(
        [corr_imag.reshape(shape_one), -corr_real.reshape(shape_one)]
    )

    density = jnp.sum(field * field * occupation, axis=(0, 4))
    domain_count = neighbours.shape[0]
    domain_ids = jnp.arange(domain_count, dtype=jnp.int32)
    own_index = lax.axis_index("dom")

    def lookup(column, index):
        return jnp.sum(jnp.where(domain_ids == index, column, 0))

    lower_owner = lookup(neighbours[:, 0], own_index)
    upper_owner = lookup(neighbours[:, 1], own_index)
    flat = density.reshape(1, slab, rows_y * cols_z)
    gathered = lax.all_to_all(
        jnp.broadcast_to(flat, (domain_count,) + flat.shape[1:]), "dom", 0, 0, tiled=True
    )
    lower_slab = select_owner(gathered, lower_owner, domain_ids).reshape(slab, rows_y, cols_z)
    upper_slab = select_owner(gathered, upper_owner, domain_ids).reshape(slab, rows_y, cols_z)
    lower_brick = lax.dynamic_slice_in_dim(lower_slab, lookup(offsets[:, 0], own_index), BUF, 1)
    upper_brick = lax.dynamic_slice_in_dim(upper_slab, lookup(offsets[:, 1], own_index), BUF, 1)
    planes = jnp.arange(BUF, dtype=jnp.float32)
    weight_low = ((planes + 1.0) / (BUF + 1.0)).reshape(1, BUF, 1)
    weight_high = ((BUF - planes) / (BUF + 1.0)).reshape(1, BUF, 1)
    low = density[:, :BUF] * weight_low + lower_brick * (1.0 - weight_low)
    high = density[:, rows_y - BUF :] * weight_high + upper_brick * (1.0 - weight_high)
    blended = jnp.concatenate([low, density[:, BUF : rows_y - BUF], high], axis=1)
    new_grid = external[0].reshape(slab, rows_y, cols_z) - xc_factor * jnp.cbrt(blended + 1e-06)
    evolved = phase_turn(field, half_step * new_grid).astype(jnp.bfloat16)
    return (evolved[None], intersection[None], new_grid.reshape(1, slab, rows_y * cols_z))


def solution(mesh):
    return jax.shard_map(
        shards,
        mesh=mesh,
        in_specs=(
            P("dom", None, "space", None, None, None),
            P("dom", None, "space", None, None, None),
            P("dom", "space", None),
            P("dom", "space", None),
            P(),
            P(),
            P(),
            P(),
        ),
        out_specs=(
            P("dom", None, "space", None, None, None),
            P("dom", None, None, None),
            P("dom", "space", None),
        ),
        check_vma=False,
    )
```

```python
import jax
import jax.numpy as jnp
from jax import lax
from jax.sharding import PartitionSpec as P

TAYLOR = 4
BUF = 4
NEAR = 4

time_step = 0.4
half_step = 0.2
xc_factor = 0.9847450218426965


def neighbour_pair(value, axis):
    devices = lax.axis_size(axis)
    up = [(i, i + 1) for i in range(devices - 1)]
    down = [(i + 1, i) for i in range(devices - 1)]
    return lax.ppermute(value, axis, up), lax.ppermute(value, axis, down)


def pieces(value):
    high = lax.reduce_precision(value, 8, 7)
    rest = value - high
    middle = lax.reduce_precision(rest, 8, 7)
    low = rest - middle
    return jnp.concatenate([high, middle, low]).astype(jnp.bfloat16)


def joined(parts, rows):
    wide = parts.astype(jnp.float32)
    return wide[:rows] + wide[rows : 2 * rows] + wide[2 * rows : 3 * rows]


def laplace(source):
    center = source[..., 1:-1, :, :, :]
    total = source[..., 2:, :, :, :] + source[..., :-2, :, :, :] - 6.0 * center
    lead = ((0, 0),) * (center.ndim - 3)
    padded = jnp.pad(center, lead + ((1, 1), (1, 1), (0, 0)))
    total = total + padded[..., 2:, 1:-1, :] + padded[..., :-2, 1:-1, :]
    total = total + padded[..., 1:-1, 2:, :] + padded[..., 1:-1, :-2, :]
    return total


def phase_turn(field, cosv, sinv):
    return jnp.stack([cosv * field[0] + sinv * field[1], cosv * field[1] - sinv * field[0]])


def kinetic_body(running, wide, inside):
    slab = running.shape[1]
    term = wide
    for order in range(1, TAYLOR + 1):
        curvature = laplace(term.astype(jnp.float32))
        factor = time_step / (2.0 * order)
        keep = inside[order : inside.shape[0] - order].reshape(-1, 1, 1, 1) * factor
        update = jnp.stack([-keep * curvature[1], keep * curvature[0]])
        skip = (update.shape[1] - slab) // 2
        running = running + update[:, skip : skip + slab]
        term = lax.optimization_barrier(update.astype(jnp.bfloat16))
    return running


def contract(left, right):
    return lax.dot_general(
        left, right, (((0,), (0,)), ((), ())), preferred_element_type=jnp.float32
    )


def overlap(start_real, start_imag, rounded):
    orbits = start_real.shape[-1]
    real = rounded[0].reshape(-1, orbits)
    imag = rounded[1].reshape(-1, orbits)
    over_real = contract(start_real, real) + contract(start_imag, imag)
    over_imag = contract(start_real, imag) - contract(start_imag, real)
    return jnp.stack([over_real, over_imag])


def scatter_sum(value, axis, groups):
    members = len(groups[0])
    parts = lax.all_to_all(value, axis, 0, 0, tiled=True, axis_index_groups=groups)
    rows = value.shape[0] // members
    return jnp.sum(parts.reshape(members, rows, -1).astype(jnp.float32), axis=0)


def gather_rows(value, axis, groups):
    members = len(groups[0])
    spread = jnp.broadcast_to(value[None], (members,) + value.shape)
    spread = lax.optimization_barrier(spread)
    out = lax.all_to_all(spread, axis, 0, 0, tiled=True, axis_index_groups=groups)
    return out.reshape(-1, value.shape[-1])


def space_sum(partial, axis):
    devices = lax.axis_size(axis)
    inner = NEAR if devices % NEAR == 0 else 1
    outer = devices // inner
    near = [[q * inner + r for r in range(inner)] for q in range(outer)]
    far = [[q * inner + r for q in range(outer)] for r in range(inner)]
    mine = scatter_sum(partial.astype(jnp.bfloat16), axis, near)
    mine = scatter_sum(mine.astype(jnp.bfloat16), axis, far)
    mine = gather_rows(mine.astype(jnp.bfloat16), axis, far)
    return gather_rows(mine, axis, near)


def high_dot(left, right):
    return jnp.dot(left, right, precision=lax.Precision.HIGHEST)


def half_dot(left, right):
    return jnp.dot(left, right, preferred_element_type=jnp.float32)


def select_owner(stacked, owner, domain_ids):
    picked = (domain_ids == owner).reshape((stacked.shape[0],) + (1,) * (stacked.ndim - 1))
    return jnp.sum(jnp.where(picked, stacked, 0.0), axis=0)


def shards(orbitals, initial, potential, external, occupation, coupling, neighbours, offsets):
    start = initial[0]
    slab, rows_y, cols_z, orbits = start.shape[1:]
    devices = lax.axis_size("space")
    place = lax.axis_index("space")
    cells_total = slab * devices * rows_y * cols_z
    shape_one = (slab, rows_y, cols_z, orbits)
    start_real = start[0].reshape(-1, orbits)
    start_imag = start[1].reshape(-1, orbits)
    low_in = jnp.full((slab,), jnp.where(place > 0, 1.0, 0.0), jnp.float32)
    high_in = jnp.full((slab,), jnp.where(place < devices - 1, 1.0, 0.0), jnp.float32)
    inside = jnp.concatenate([low_in, jnp.ones((slab,), jnp.float32), high_in])

    flat_rows = 2 * slab * rows_y * cols_z
    spare = -3 * slab % 16
    extra = jnp.pad(pieces(potential[0]), ((0, spare), (0, 0)))
    message = jnp.concatenate([start.reshape(flat_rows, orbits), extra])
    below, above = neighbour_pair(message, "space")
    field_below, field_above = neighbour_pair(orbitals[0], "space")
    full = (2,) + shape_one
    wide_start = jnp.concatenate(
        [below[:flat_rows].reshape(full), start, above[:flat_rows].reshape(full)], axis=1
    ).astype(jnp.float32)
    wide_field = jnp.concatenate([field_below, orbitals[0], field_above], axis=1)
    wide_field = wide_field.astype(jnp.float32)
    wide_potential = jnp.concatenate(
        [joined(below[flat_rows:], slab), potential[0], joined(above[flat_rows:], slab)]
    )
    angle = half_step * wide_potential.reshape(3 * slab, rows_y, cols_z)
    cosv = jnp.cos(angle)[..., None]
    sinv = jnp.sin(angle)[..., None]
    own = slice(slab, 2 * slab)

    def evolve(turned_wide):
        sent = lax.optimization_barrier(turned_wide.astype(jnp.bfloat16))
        moved = kinetic_body(turned_wide[:, own], sent, inside)
        return phase_turn(moved, cosv[own], sinv[own])

    part_real = evolve(jnp.stack([cosv * wide_start[0], -sinv * wide_start[0]]))
    part_imag = evolve(jnp.stack([cosv * wide_start[1], -sinv * wide_start[1]]))
    moved = jnp.stack([part_real[0] - part_imag[1], part_real[1] + part_imag[0]])
    adjoint = jnp.stack([part_real[0] + part_imag[1], part_imag[0] - part_real[1]])
    moved = lax.optimization_barrier(moved.astype(jnp.bfloat16))
    adjoint = lax.optimization_barrier(adjoint.astype(jnp.bfloat16))
    first = evolve(phase_turn(wide_field, cosv, sinv))
    turned = phase_turn(first, cosv[own], sinv[own])
    sent = lax.optimization_barrier(turned.astype(jnp.bfloat16))
    sent_below, sent_above = neighbour_pair(sent, "space")
    rounded = first.astype(jnp.bfloat16)
    partial = jnp.concatenate(
        [
            overlap(start_real, start_imag, rounded),
            overlap(adjoint[0].reshape(-1, orbits), adjoint[1].reshape(-1, orbits), rounded),
            overlap(start_real, start_imag, moved),
        ]
    ) * (1.0 / cells_total)
    wide = jnp.concatenate([sent_below, sent, sent_above], axis=1)
    second = phase_turn(kinetic_body(turned, wide, inside), cosv[own], sinv[own])
    summed = space_sum(partial.reshape(-1, orbits), "space").reshape(6, orbits, orbits)
    wide_sum = summed.astype(jnp.float32)
    mix1_real = high_dot(coupling, wide_sum[0]).astype(jnp.bfloat16)
    mix1_imag = high_dot(coupling, wide_sum[1]).astype(jnp.bfloat16)
    gram_real, gram_imag = summed[4], summed[5]
    over_real = wide_sum[2] + time_step * (
        half_dot(gram_real, mix1_imag) + half_dot(gram_imag, mix1_real)
    )
    over_imag = wide_sum[3] - time_step * (
        half_dot(gram_real, mix1_real) - half_dot(gram_imag, mix1_imag)
    )
    intersection = jnp.stack([over_real, over_imag])
    mix2_real = high_dot(coupling, over_real).astype(jnp.bfloat16)
    mix2_imag = high_dot(coupling, over_imag).astype(jnp.bfloat16)
    moved_real = moved[0].reshape(-1, orbits)
    moved_imag = moved[1].reshape(-1, orbits)
    corr_real = (
        half_dot(moved_real, mix1_real)
        - half_dot(moved_imag, mix1_imag)
        + half_dot(start_real, mix2_real)
        - half_dot(start_imag, mix2_imag)
    )
    corr_imag = (
        half_dot(moved_real, mix1_imag)
        + half_dot(moved_imag, mix1_real)
        + half_dot(start_real, mix2_imag)
        + half_dot(start_imag, mix2_real)
    )
    field = second + time_step * jnp.stack(
        [corr_imag.reshape(shape_one), -corr_real.reshape(shape_one)]
    )

    density = jnp.sum(field * field * occupation, axis=(0, 4))
    domain_count = neighbours.shape[0]
    domain_ids = jnp.arange(domain_count, dtype=jnp.int32)
    own_index = lax.axis_index("dom")

    def lookup(column, index):
        return jnp.sum(jnp.where(domain_ids == index, column, 0))

    lower_owner = lookup(neighbours[:, 0], own_index)
    upper_owner = lookup(neighbours[:, 1], own_index)
    flat = density.reshape(1, slab, rows_y * cols_z)
    gathered = lax.all_to_all(
        jnp.broadcast_to(flat, (domain_count,) + flat.shape[1:]), "dom", 0, 0, tiled=True
    )
    lower_slab = select_owner(gathered, lower_owner, domain_ids).reshape(slab, rows_y, cols_z)
    upper_slab = select_owner(gathered, upper_owner, domain_ids).reshape(slab, rows_y, cols_z)
    lower_brick = lax.dynamic_slice_in_dim(lower_slab, lookup(offsets[:, 0], own_index), BUF, 1)
    upper_brick = lax.dynamic_slice_in_dim(upper_slab, lookup(offsets[:, 1], own_index), BUF, 1)
    planes = jnp.arange(BUF, dtype=jnp.float32)
    weight_low = ((planes + 1.0) / (BUF + 1.0)).reshape(1, BUF, 1)
    weight_high = ((BUF - planes) / (BUF + 1.0)).reshape(1, BUF, 1)
    low = density[:, :BUF] * weight_low + lower_brick * (1.0 - weight_low)
    high = density[:, rows_y - BUF :] * weight_high + upper_brick * (1.0 - weight_high)
    blended = jnp.concatenate([low, density[:, BUF : rows_y - BUF], high], axis=1)
    new_grid = external[0].reshape(slab, rows_y, cols_z) - xc_factor * jnp.cbrt(blended + 1e-06)
    turn = (half_step * new_grid)[..., None]
    evolved = phase_turn(field, jnp.cos(turn), jnp.sin(turn)).astype(jnp.bfloat16)
    return (evolved[None], intersection[None], new_grid.reshape(1, slab, rows_y * cols_z))


def solution(mesh):
    return jax.shard_map(
        shards,
        mesh=mesh,
        in_specs=(
            P("dom", None, "space", None, None, None),
            P("dom", None, "space", None, None, None),
            P("dom", "space", None),
            P("dom", "space", None),
            P(),
            P(),
            P(),
            P(),
        ),
        out_specs=(
            P("dom", None, "space", None, None, None),
            P("dom", None, None, None),
            P("dom", "space", None),
        ),
        check_vma=False,
    )
```

```python
import jax
import jax.numpy as jnp
from jax import lax
from jax.experimental import pallas as pl
from jax.experimental.pallas import tpu as pltpu
from jax.sharding import PartitionSpec as P

TAYLOR = 4
BUF = 4

time_step = 0.4
half_step = 0.2
xc_factor = 0.9847450218426965


def neighbour_pair(value, axis):
    devices = lax.axis_size(axis)
    up = [(i, i + 1) for i in range(devices - 1)]
    down = [(i + 1, i) for i in range(devices - 1)]
    return lax.ppermute(value, axis, up), lax.ppermute(value, axis, down)


def rounded(value):
    return value.astype(jnp.bfloat16).astype(jnp.float32)


def spread_column(row):
    return jnp.broadcast_to(row, (row.shape[-1], row.shape[-1])).T


def laplace(ref, part, plane):
    center = ref[part, plane]
    side = center.shape[1]
    zero = jnp.zeros((1,) + center.shape[1:], jnp.float32)
    total = ref[part, plane - 1] + ref[part, plane + 1]
    total = total + jnp.concatenate([center[1:], zero]) + jnp.concatenate([zero, center[:-1]])
    level = lax.broadcasted_iota(jnp.int32, center.shape, 1)
    total = total + jnp.where(level == side - 1, 0.0, pltpu.roll(center, side - 1, 1))
    total = total + jnp.where(level == 0, 0.0, pltpu.roll(center, 1, 1))
    return total - 6.0 * center


def kinetic(edge, running, even, odd, slab, grid):
    planes = 3 * slab
    cells = grid[0] * grid[1]
    now, after = even, odd
    for order in range(1, TAYLOR + 1):
        factor = time_step / (2.0 * order)

        def one(plane, carry, now=now, after=after, factor=factor, last=order == TAYLOR):
            inside = jnp.where(plane < slab, edge[0], jnp.where(plane >= 2 * slab, edge[1], 1.0))
            keep = inside * factor
            real = -keep * laplace(now, 1, plane)
            imag = keep * laplace(now, 0, plane)
            for part, update in enumerate((real, imag)):
                running[part, plane] = running[part, plane] + update
                if not last:
                    flat = update.reshape(cells, update.shape[-1])
                    after[part, plane] = rounded(flat).reshape(update.shape)
            return carry

        lax.fori_loop(order, planes - order, one, 0)
        now, after = after, now


def fill_phase(potential, row, place, cos_ref, sin_ref, slab):
    cosv = jnp.cos(half_step * potential)
    sinv = jnp.sin(half_step * potential)
    for plane in range(slab):
        cos_ref[place + plane] = spread_column(cosv[row + plane : row + plane + 1])
        sin_ref[place + plane] = spread_column(sinv[row + plane : row + plane + 1])


def front_kernel(slab, grid, scale, edge, low_i, own_i, high_i, low_o, own_o, high_o, pot,
                 partial_ref, moved_ref, sent_ref, turned_ref,
                 even, odd, running, cos_ref, sin_ref, part_ref, adjoint_ref, right):
    cells = grid[0] * grid[1]
    half = slab * cells
    lanes = own_i.shape[-1]
    tail = 2 * half
    box = grid + (lanes,)
    for group, ref in ((0, low_i), (2, high_i)):
        extra = ref[tail : tail + 32].astype(jnp.float32)
        whole = extra[0:8] + extra[8:16] + extra[16:24]
        fill_phase(whole, 0, group * slab, cos_ref, sin_ref, slab)
    fill_phase(pot[...], 0, slab, cos_ref, sin_ref, slab)

    def start_at(plane, real, imag):
        for part, value in enumerate((real, imag)):
            running[part, plane] = value.reshape(box)
            even[part, plane] = rounded(value).reshape(box)

    def load(ref, part, plane):
        at = pl.multiple_of((part * slab + plane) * cells, cells)
        return ref[pl.ds(at, cells), :].astype(jnp.float32)

    def finish(plane):
        real = running[0, slab + plane].reshape(cells, lanes)
        imag = running[1, slab + plane].reshape(cells, lanes)
        cosv = cos_ref[slab + plane]
        sinv = sin_ref[slab + plane]
        return cosv * real + sinv * imag, cosv * imag - sinv * real

    for part in range(2):
        for group, ref in enumerate((low_i, own_i, high_i)):

            def begin(plane, carry, ref=ref, group=group, part=part):
                value = load(ref, part, plane)
                at = group * slab + plane
                start_at(at, cos_ref[at] * value, -sin_ref[at] * value)
                return carry

            lax.fori_loop(0, slab, begin, 0)
        kinetic(edge, running, even, odd, slab, grid)
        for plane in range(slab):
            real, imag = finish(plane)
            low = plane * cells
            if part == 0:
                part_ref[0, plane] = real
                part_ref[1, plane] = imag
            else:
                kept_real = part_ref[0, plane]
                kept_imag = part_ref[1, plane]
                moved_real = (kept_real - imag).astype(jnp.bfloat16)
                moved_imag = (kept_imag + real).astype(jnp.bfloat16)
                moved_ref[low : low + cells] = moved_real
                moved_ref[half + low : half + low + cells] = moved_imag
                right[low : low + cells, 2 * lanes : 3 * lanes] = moved_real
                right[low : low + cells, 3 * lanes :] = moved_imag
                right[half + low : half + low + cells, 2 * lanes : 3 * lanes] = moved_imag
                right[half + low : half + low + cells, 3 * lanes :] = -moved_real
                adjoint_ref[low : low + cells] = (kept_real + imag).astype(jnp.bfloat16)
                adjoint_ref[half + low : half + low + cells] = (real - kept_imag).astype(jnp.bfloat16)

    for group, ref in enumerate((low_o, own_o, high_o)):

        def begin_field(plane, carry, ref=ref, group=group):
            real = load(ref, 0, plane)
            imag = load(ref, 1, plane)
            at = group * slab + plane
            cosv = cos_ref[at]
            sinv = sin_ref[at]
            start_at(at, cosv * real + sinv * imag, cosv * imag - sinv * real)
            return carry

        lax.fori_loop(0, slab, begin_field, 0)
    kinetic(edge, running, even, odd, slab, grid)
    for plane in range(slab):
        real, imag = finish(plane)
        low = plane * cells
        cosv = cos_ref[slab + plane]
        sinv = sin_ref[slab + plane]
        turned_real = cosv * real + sinv * imag
        turned_imag = cosv * imag - sinv * real
        turned_ref[low : low + cells] = turned_real
        turned_ref[half + low : half + low + cells] = turned_imag
        sent_ref[low : low + cells] = turned_real.astype(jnp.bfloat16)
        sent_ref[half + low : half + low + cells] = turned_imag.astype(jnp.bfloat16)
        first_real = real.astype(jnp.bfloat16)
        first_imag = imag.astype(jnp.bfloat16)
        right[low : low + cells, :lanes] = first_real
        right[low : low + cells, lanes : 2 * lanes] = first_imag
        right[half + low : half + low + cells, :lanes] = first_imag
        right[half + low : half + low + cells, lanes : 2 * lanes] = -first_real

    over = contract(own_i[...], right[...]) * scale
    cross = contract(adjoint_ref[...], right[:, : 2 * lanes]) * scale
    for index in range(2):
        piece = slice(index * lanes, (index + 1) * lanes)
        partial_ref[index * lanes : (index + 1) * lanes] = over[:, piece].astype(jnp.bfloat16)
        partial_ref[(2 + index) * lanes : (3 + index) * lanes] = cross[:, piece].astype(jnp.bfloat16)
        piece = slice((2 + index) * lanes, (3 + index) * lanes)
        partial_ref[(4 + index) * lanes : (5 + index) * lanes] = over[:, piece].astype(jnp.bfloat16)


def second_kernel(slab, grid, edge, low, own, high, turned, pot, second_ref,
                  even, odd, running, cos_ref, sin_ref):
    cells = grid[0] * grid[1]
    half = slab * cells
    lanes = own.shape[-1]
    box = grid + (lanes,)
    fill_phase(pot[...], 0, 0, cos_ref, sin_ref, slab)
    for part in range(2):
        for group, ref in enumerate((low, own, high)):

            def begin(plane, carry, ref=ref, group=group, part=part):
                at = pl.multiple_of((part * slab + plane) * cells, cells)
                value = ref[pl.ds(at, cells), :].astype(jnp.float32).reshape(box)
                even[part, group * slab + plane] = value
                if group == 1:
                    running[part, slab + plane] = turned[pl.ds(at, cells), :].reshape(box)
                return carry

            lax.fori_loop(0, slab, begin, 0)
    kinetic(edge, running, even, odd, slab, grid)
    for plane in range(slab):
        real = running[0, slab + plane].reshape(cells, lanes)
        imag = running[1, slab + plane].reshape(cells, lanes)
        cosv = cos_ref[plane]
        sinv = sin_ref[plane]
        at = plane * cells
        second_ref[at : at + cells] = cosv * real + sinv * imag
        second_ref[half + at : half + at + cells] = cosv * imag - sinv * real


def sum_kernel(parts_ref, out_ref):
    total = parts_ref[0].astype(jnp.float32)
    for index in range(1, parts_ref.shape[0]):
        total = total + parts_ref[index].astype(jnp.float32)
    total = total.astype(jnp.bfloat16)
    for index in range(out_ref.shape[0]):
        out_ref[index] = total


def back_kernel(slab, sums, coupling, moved, start, second, occupation,
                inter_ref, field_ref, density_ref):
    lanes = coupling.shape[-1]
    half = start.shape[0] // 2
    cells = half // slab
    strength = coupling[...]

    def matrix(index):
        return sums[index * lanes : (index + 1) * lanes]

    def mixed(real, imag):
        return (
            high_dot(strength, real).astype(jnp.bfloat16),
            high_dot(strength, imag).astype(jnp.bfloat16),
        )

    mix1_real, mix1_imag = mixed(
        matrix(0).astype(jnp.float32), matrix(1).astype(jnp.float32)
    )
    gram_real, gram_imag = matrix(4), matrix(5)
    over_real = matrix(2).astype(jnp.float32) + time_step * (
        half_dot(gram_real, mix1_imag) + half_dot(gram_imag, mix1_real)
    )
    over_imag = matrix(3).astype(jnp.float32) - time_step * (
        half_dot(gram_real, mix1_real) - half_dot(gram_imag, mix1_imag)
    )
    inter_ref[:lanes] = over_real
    inter_ref[lanes:] = over_imag
    mix2_real, mix2_imag = mixed(over_real, over_imag)
    mix1_real_imag = jnp.concatenate([mix1_real, mix1_imag], axis=1)
    mix1_turned = jnp.concatenate([-mix1_imag, mix1_real], axis=1)
    mix2_real_imag = jnp.concatenate([mix2_real, mix2_imag], axis=1)
    mix2_turned = jnp.concatenate([-mix2_imag, mix2_real], axis=1)
    weight = jnp.broadcast_to(occupation[...], (8, lanes))
    for plane in range(slab):
        low = plane * cells
        real_rows = slice(low, low + cells)
        imag_rows = slice(half + low, half + low + cells)
        corr = (
            half_dot(moved[real_rows], mix1_real_imag)
            + half_dot(moved[imag_rows], mix1_turned)
            + half_dot(start[real_rows], mix2_real_imag)
            + half_dot(start[imag_rows], mix2_turned)
        )
        real = second[real_rows] + time_step * corr[:, lanes:]
        imag = second[imag_rows] - time_step * corr[:, :lanes]
        field_ref[real_rows] = real
        field_ref[imag_rows] = imag
        square = real * real + imag * imag
        dense = lax.dot_general(
            weight,
            square,
            (((1,), (1,)), ((), ())),
            precision=lax.Precision.HIGHEST,
            preferred_element_type=jnp.float32,
        )
        for owner in range(density_ref.shape[0]):
            density_ref[owner, plane : plane + 1] = dense[:1]


def tail_kernel(slab, grid, place, gathered, external, field, grid_ref, evolved_ref):
    lanes = external.shape[-1]
    half = field.shape[0] // 2
    cells = half // slab
    side = grid[1]
    own = gathered[place[4]]
    lower = gathered[place[0]]
    upper = gathered[place[1]]
    lower = pltpu.roll(lower, (lanes - place[2] * side) % lanes, 1)
    upper = pltpu.roll(upper, (2 * lanes - BUF * side - place[3] * side) % lanes, 1)
    level = lax.broadcasted_iota(jnp.int32, own.shape, 1) // side
    step = level.astype(jnp.float32)
    weight_low = (step + 1.0) / (BUF + 1.0)
    weight_high = (grid[0] - step) / (BUF + 1.0)
    low = own * weight_low + lower * (1.0 - weight_low)
    high = own * weight_high + upper * (1.0 - weight_high)
    blended = jnp.where(level < BUF, low, jnp.where(level >= grid[0] - BUF, high, own))
    root = jnp.exp(jnp.log(blended + 1e-06) * (1.0 / 3.0))
    new_grid = external[...] - xc_factor * root
    grid_ref[...] = new_grid
    cosv = jnp.cos(half_step * new_grid)
    sinv = jnp.sin(half_step * new_grid)
    for plane in range(slab):
        low_row = plane * cells
        real = field[low_row : low_row + cells]
        imag = field[half + low_row : half + low_row + cells]
        cos_b = spread_column(cosv[plane : plane + 1])
        sin_b = spread_column(sinv[plane : plane + 1])
        evolved_ref[low_row : low_row + cells] = (cos_b * real + sin_b * imag).astype(jnp.bfloat16)
        evolved_ref[half + low_row : half + low_row + cells] = (
            cos_b * imag - sin_b * real
        ).astype(jnp.bfloat16)


def contract(left, right):
    return lax.dot_general(
        left, right, (((0,), (0,)), ((), ())), preferred_element_type=jnp.float32
    )


def high_dot(left, right):
    return jnp.dot(
        left, right, precision=lax.Precision.HIGHEST, preferred_element_type=jnp.float32
    )


def half_dot(left, right):
    return jnp.dot(left, right, preferred_element_type=jnp.float32)


def pieces(value):
    high = lax.reduce_precision(value, 8, 7)
    rest = value - high
    middle = lax.reduce_precision(rest, 8, 7)
    low = rest - middle
    rows = value.shape[0]
    pad = jnp.zeros((8 - rows,) + value.shape[1:], value.dtype)
    stacked = jnp.concatenate([high, pad, middle, pad, low, pad, jnp.zeros((8,) + value.shape[1:])])
    return stacked.astype(jnp.bfloat16)


def scalars(count):
    return [pl.BlockSpec(memory_space=pltpu.SMEM)] + [
        pl.BlockSpec(memory_space=pltpu.VMEM) for _ in range(count)
    ]


def shards(orbitals, initial, potential, external, occupation, coupling, neighbours, offsets):
    slab, rows_y, cols_z, orbits = initial.shape[2:]
    grid = (rows_y, cols_z)
    cells = rows_y * cols_z
    rows = 2 * slab * cells
    start = initial.reshape(rows, orbits)
    devices = lax.axis_size("space")
    place = lax.axis_index("space")
    f32, bf16 = jnp.float32, jnp.bfloat16
    edge = jnp.stack([place > 0, place < devices - 1]).astype(f32)
    planes = (2, 3 * slab) + grid + (orbits,)
    stencil = [pltpu.VMEM(planes, f32) for _ in range(3)]
    message = jnp.concatenate([start, pieces(potential[0])])
    orbs = orbitals.reshape(rows, orbits)
    low_i, high_i = neighbour_pair(message, "space")
    low_o, high_o = neighbour_pair(orbs, "space")
    scale = 1.0 / (slab * devices * cells)
    shape = jax.ShapeDtypeStruct
    partial, moved, sent, turned = pl.pallas_call(
        lambda *refs: front_kernel(slab, grid, scale, *refs),
        out_shape=(
            shape((6 * orbits, orbits), bf16),
            shape((rows, orbits), bf16),
            shape((rows, orbits), bf16),
            shape((rows, orbits), f32),
        ),
        in_specs=scalars(7),
        scratch_shapes=stencil
        + [pltpu.VMEM((3 * slab, cells, orbits), f32) for _ in range(2)]
        + [
            pltpu.VMEM((2, slab, cells, orbits), f32),
            pltpu.VMEM((rows, orbits), bf16),
            pltpu.VMEM((rows, 4 * orbits), bf16),
        ],
        compiler_params=pltpu.CompilerParams(vmem_limit_bytes=20 << 20),
        name="front",
    )(edge, low_i, start, high_i, low_o, orbs, high_o, potential[0])

    share = 6 * orbits // devices
    parts = lax.all_to_all(partial.reshape(devices, share, orbits), "space", 0, 0, tiled=True)
    low_s, high_s = neighbour_pair(sent, "space")
    spread = pl.pallas_call(
        sum_kernel,
        out_shape=shape((devices, share, orbits), bf16),
        compiler_params=pltpu.CompilerParams(vmem_limit_bytes=6 << 20),
        name="total",
    )(parts)
    sums = lax.all_to_all(spread, "space", 0, 0, tiled=True).reshape(6 * orbits, orbits)
    second = pl.pallas_call(
        lambda *refs: second_kernel(slab, grid, *refs),
        out_shape=shape((rows, orbits), f32),
        in_specs=scalars(5),
        scratch_shapes=stencil + [pltpu.VMEM((slab, cells, orbits), f32) for _ in range(2)],
        compiler_params=pltpu.CompilerParams(vmem_limit_bytes=14 << 20),
        name="second",
    )(edge, low_s, sent, high_s, turned, potential[0])

    domain_count = neighbours.shape[0]
    intersection, field, density = pl.pallas_call(
        lambda *refs: back_kernel(slab, *refs),
        out_shape=(
            shape((2 * orbits, orbits), f32),
            shape((rows, orbits), f32),
            shape((domain_count, slab, cells), f32),
        ),
        compiler_params=pltpu.CompilerParams(vmem_limit_bytes=14 << 20),
        name="back",
    )(sums, coupling, moved, start, second, occupation.reshape(1, orbits))
    gathered = lax.all_to_all(density, "dom", 0, 0, tiled=True)
    own_index = lax.axis_index("dom")
    mine = lax.dynamic_index_in_dim(neighbours, own_index, 0, keepdims=False)
    shift = lax.dynamic_index_in_dim(offsets, own_index, 0, keepdims=False)
    where = jnp.concatenate([mine, shift, own_index.reshape(1).astype(jnp.int32)])
    new_grid, evolved = pl.pallas_call(
        lambda *refs: tail_kernel(slab, grid, *refs),
        out_shape=(shape((slab, cells), f32), shape((rows, orbits), bf16)),
        in_specs=scalars(3),
        compiler_params=pltpu.CompilerParams(vmem_limit_bytes=8 << 20),
        name="tail",
    )(where, gathered, external[0], field)
    return (
        evolved.reshape(orbitals.shape),
        intersection.reshape(1, 2, orbits, orbits),
        new_grid[None],
    )


def solution(mesh):
    return jax.shard_map(
        shards,
        mesh=mesh,
        in_specs=(
            P("dom", None, "space", None, None, None),
            P("dom", None, "space", None, None, None),
            P("dom", "space", None),
            P("dom", "space", None),
            P(),
            P(),
            P(),
            P(),
        ),
        out_specs=(
            P("dom", None, "space", None, None, None),
            P("dom", None, None, None),
            P("dom", "space", None),
        ),
        check_vma=False,
    )
```

```python
import jax
import jax.numpy as jnp
from jax import lax
from jax.experimental import pallas as pl
from jax.experimental.pallas import tpu as pltpu
from jax.sharding import PartitionSpec as P


TAYLOR = 4
BUF = 4

time_step = 0.4
half_step = 0.2
xc_factor = 0.9847450218426965


def neighbour_pair(value, axis):
    devices = lax.axis_size(axis)
    up = [(i, i + 1) for i in range(devices - 1)]
    down = [(i + 1, i) for i in range(devices - 1)]
    return lax.ppermute(value, axis, up), lax.ppermute(value, axis, down)


def rounded(value):
    return value.astype(jnp.bfloat16).astype(jnp.float32)


def spread_column(row):
    return jnp.broadcast_to(row, (row.shape[-1], row.shape[-1])).T


def laplace(ref, part, plane):
    center = ref[part, plane]
    side = center.shape[1]
    zero = jnp.zeros((1,) + center.shape[1:], jnp.float32)
    total = ref[part, plane - 1] + ref[part, plane + 1]
    total = total + jnp.concatenate([center[1:], zero]) + jnp.concatenate([zero, center[:-1]])
    level = lax.broadcasted_iota(jnp.int32, center.shape, 1)
    total = total + jnp.where(level == side - 1, 0.0, pltpu.roll(center, side - 1, 1))
    total = total + jnp.where(level == 0, 0.0, pltpu.roll(center, 1, 1))
    return total - 6.0 * center


def kinetic(edge, running, even, odd, slab, grid):
    planes = 3 * slab
    cells = grid[0] * grid[1]
    now, after = even, odd
    for order in range(1, TAYLOR + 1):
        factor = time_step / (2.0 * order)

        def one(plane, carry, now=now, after=after, factor=factor, last=order == TAYLOR):
            inside = jnp.where(plane < slab, edge[0], jnp.where(plane >= 2 * slab, edge[1], 1.0))
            keep = inside * factor
            real = -keep * laplace(now, 1, plane)
            imag = keep * laplace(now, 0, plane)
            for part, update in enumerate((real, imag)):
                running[part, plane] = running[part, plane] + update
                if not last:
                    flat = update.reshape(cells, update.shape[-1])
                    after[part, plane] = rounded(flat).reshape(update.shape)
            return carry

        lax.fori_loop(order, planes - order, one, 0)
        now, after = after, now


def fill_phase(potential, row, place, cos_ref, sin_ref, slab):
    cosv = jnp.cos(half_step * potential)
    sinv = jnp.sin(half_step * potential)
    for plane in range(slab):
        cos_ref[place + plane] = spread_column(cosv[row + plane : row + plane + 1])
        sin_ref[place + plane] = spread_column(sinv[row + plane : row + plane + 1])


def front_kernel(slab, grid, scale, edge, low_ref, own_ref, high_ref, pot,
                 partial_ref, moved_ref, sent_ref, turned_ref,
                 even, odd, running, cos_ref, sin_ref, part_ref, adjoint_ref, right):
    cells = grid[0] * grid[1]
    half = slab * cells
    lanes = own_ref.shape[-1]
    tail = 4 * half
    box = grid + (lanes,)
    for group, ref in ((0, low_ref), (2, high_ref)):
        extra = ref[tail : tail + 32].astype(jnp.float32)
        whole = extra[0:8] + extra[8:16] + extra[16:24]
        fill_phase(whole, 0, group * slab, cos_ref, sin_ref, slab)
    fill_phase(pot[...], 0, slab, cos_ref, sin_ref, slab)

    def start_at(plane, real, imag):
        for part, value in enumerate((real, imag)):
            running[part, plane] = value.reshape(box)
            even[part, plane] = rounded(value).reshape(box)

    def load(ref, part, plane):
        at = pl.multiple_of((part * slab + plane) * cells, cells)
        return ref[pl.ds(at, cells), :].astype(jnp.float32)

    def finish(plane):
        real = running[0, slab + plane].reshape(cells, lanes)
        imag = running[1, slab + plane].reshape(cells, lanes)
        cosv = cos_ref[slab + plane]
        sinv = sin_ref[slab + plane]
        return cosv * real + sinv * imag, cosv * imag - sinv * real

    for part in range(2):
        for group, ref in enumerate((low_ref, own_ref, high_ref)):

            def begin(plane, carry, ref=ref, group=group, part=part):
                value = load(ref, part, plane)
                at = group * slab + plane
                start_at(at, cos_ref[at] * value, -sin_ref[at] * value)
                return carry

            lax.fori_loop(0, slab, begin, 0)
        kinetic(edge, running, even, odd, slab, grid)
        for plane in range(slab):
            real, imag = finish(plane)
            low = plane * cells
            if part == 0:
                part_ref[0, plane] = real
                part_ref[1, plane] = imag
            else:
                kept_real = part_ref[0, plane]
                kept_imag = part_ref[1, plane]
                moved_real = (kept_real - imag).astype(jnp.bfloat16)
                moved_imag = (kept_imag + real).astype(jnp.bfloat16)
                moved_ref[low : low + cells] = moved_real
                moved_ref[half + low : half + low + cells] = moved_imag
                right[low : low + cells, 2 * lanes : 3 * lanes] = moved_real
                right[low : low + cells, 3 * lanes :] = moved_imag
                right[half + low : half + low + cells, 2 * lanes : 3 * lanes] = moved_imag
                right[half + low : half + low + cells, 3 * lanes :] = -moved_real
                adjoint_ref[low : low + cells] = (kept_real + imag).astype(jnp.bfloat16)
                adjoint_ref[half + low : half + low + cells] = (real - kept_imag).astype(jnp.bfloat16)

    for group, ref in enumerate((low_ref, own_ref, high_ref)):

        def begin_field(plane, carry, ref=ref, group=group):
            real = load(ref, 2, plane)
            imag = load(ref, 3, plane)
            at = group * slab + plane
            cosv = cos_ref[at]
            sinv = sin_ref[at]
            start_at(at, cosv * real + sinv * imag, cosv * imag - sinv * real)
            return carry

        lax.fori_loop(0, slab, begin_field, 0)
    kinetic(edge, running, even, odd, slab, grid)
    for plane in range(slab):
        real, imag = finish(plane)
        low = plane * cells
        cosv = cos_ref[slab + plane]
        sinv = sin_ref[slab + plane]
        turned_real = cosv * real + sinv * imag
        turned_imag = cosv * imag - sinv * real
        turned_ref[low : low + cells] = turned_real
        turned_ref[half + low : half + low + cells] = turned_imag
        sent_ref[low : low + cells] = turned_real.astype(jnp.bfloat16)
        sent_ref[half + low : half + low + cells] = turned_imag.astype(jnp.bfloat16)
        first_real = real.astype(jnp.bfloat16)
        first_imag = imag.astype(jnp.bfloat16)
        right[low : low + cells, :lanes] = first_real
        right[low : low + cells, lanes : 2 * lanes] = first_imag
        right[half + low : half + low + cells, :lanes] = first_imag
        right[half + low : half + low + cells, lanes : 2 * lanes] = -first_real

    over = contract(own_ref[: 2 * half], right[...]) * scale
    cross = contract(adjoint_ref[...], right[:, : 2 * lanes]) * scale
    for index in range(2):
        piece = slice(index * lanes, (index + 1) * lanes)
        partial_ref[index * lanes : (index + 1) * lanes] = over[:, piece].astype(jnp.bfloat16)
        partial_ref[(2 + index) * lanes : (3 + index) * lanes] = cross[:, piece].astype(jnp.bfloat16)
        piece = slice((2 + index) * lanes, (3 + index) * lanes)
        partial_ref[(4 + index) * lanes : (5 + index) * lanes] = over[:, piece].astype(jnp.bfloat16)


def second_kernel(slab, grid, edge, low, own, high, turned, pot, second_ref,
                  even, odd, running, cos_ref, sin_ref):
    cells = grid[0] * grid[1]
    half = slab * cells
    lanes = own.shape[-1]
    box = grid + (lanes,)
    fill_phase(pot[...], 0, 0, cos_ref, sin_ref, slab)
    for part in range(2):
        for group, ref in enumerate((low, own, high)):

            def begin(plane, carry, ref=ref, group=group, part=part):
                at = pl.multiple_of((part * slab + plane) * cells, cells)
                value = ref[pl.ds(at, cells), :].astype(jnp.float32).reshape(box)
                even[part, group * slab + plane] = value
                if group == 1:
                    running[part, slab + plane] = turned[pl.ds(at, cells), :].reshape(box)
                return carry

            lax.fori_loop(0, slab, begin, 0)
    kinetic(edge, running, even, odd, slab, grid)
    for plane in range(slab):
        real = running[0, slab + plane].reshape(cells, lanes)
        imag = running[1, slab + plane].reshape(cells, lanes)
        cosv = cos_ref[plane]
        sinv = sin_ref[plane]
        at = plane * cells
        second_ref[at : at + cells] = cosv * real + sinv * imag
        second_ref[half + at : half + at + cells] = cosv * imag - sinv * real


def sum_kernel(parts_ref, out_ref):
    total = parts_ref[0].astype(jnp.float32)
    for index in range(1, parts_ref.shape[0]):
        total = total + parts_ref[index].astype(jnp.float32)
    total = total.astype(jnp.bfloat16)
    for index in range(out_ref.shape[0]):
        out_ref[index] = total


def back_kernel(slab, sums, coupling, moved, start, second, occupation,
                inter_ref, field_ref, density_ref):
    lanes = coupling.shape[-1]
    half = start.shape[0] // 2
    cells = half // slab
    strength = coupling[...]

    def matrix(index):
        return sums[index * lanes : (index + 1) * lanes]

    def mixed(real, imag):
        return (
            high_dot(strength, real).astype(jnp.bfloat16),
            high_dot(strength, imag).astype(jnp.bfloat16),
        )

    mix1_real, mix1_imag = mixed(
        matrix(0).astype(jnp.float32), matrix(1).astype(jnp.float32)
    )
    gram_real, gram_imag = matrix(4), matrix(5)
    over_real = matrix(2).astype(jnp.float32) + time_step * (
        half_dot(gram_real, mix1_imag) + half_dot(gram_imag, mix1_real)
    )
    over_imag = matrix(3).astype(jnp.float32) - time_step * (
        half_dot(gram_real, mix1_real) - half_dot(gram_imag, mix1_imag)
    )
    inter_ref[:lanes] = over_real
    inter_ref[lanes:] = over_imag
    mix2_real, mix2_imag = mixed(over_real, over_imag)
    mix1_real_imag = jnp.concatenate([mix1_real, mix1_imag], axis=1)
    mix1_turned = jnp.concatenate([-mix1_imag, mix1_real], axis=1)
    mix2_real_imag = jnp.concatenate([mix2_real, mix2_imag], axis=1)
    mix2_turned = jnp.concatenate([-mix2_imag, mix2_real], axis=1)
    weight = jnp.broadcast_to(occupation[...], (8, lanes))
    for plane in range(slab):
        low = plane * cells
        real_rows = slice(low, low + cells)
        imag_rows = slice(half + low, half + low + cells)
        corr = (
            half_dot(moved[real_rows], mix1_real_imag)
            + half_dot(moved[imag_rows], mix1_turned)
            + half_dot(start[real_rows], mix2_real_imag)
            + half_dot(start[imag_rows], mix2_turned)
        )
        real = second[real_rows] + time_step * corr[:, lanes:]
        imag = second[imag_rows] - time_step * corr[:, :lanes]
        field_ref[real_rows] = real
        field_ref[imag_rows] = imag
        square = real * real + imag * imag
        dense = lax.dot_general(
            weight,
            square,
            (((1,), (1,)), ((), ())),
            precision=lax.Precision.HIGHEST,
            preferred_element_type=jnp.float32,
        )
        for owner in range(density_ref.shape[0]):
            density_ref[owner, plane : plane + 1] = dense[:1]


def tail_kernel(slab, grid, place, gathered, external, field, grid_ref, evolved_ref):
    lanes = external.shape[-1]
    half = field.shape[0] // 2
    cells = half // slab
    side = grid[1]
    own = gathered[place[4]]
    lower = gathered[place[0]]
    upper = gathered[place[1]]
    lower = pltpu.roll(lower, (lanes - place[2] * side) % lanes, 1)
    upper = pltpu.roll(upper, (2 * lanes - BUF * side - place[3] * side) % lanes, 1)
    level = lax.broadcasted_iota(jnp.int32, own.shape, 1) // side
    step = level.astype(jnp.float32)
    weight_low = (step + 1.0) / (BUF + 1.0)
    weight_high = (grid[0] - step) / (BUF + 1.0)
    low = own * weight_low + lower * (1.0 - weight_low)
    high = own * weight_high + upper * (1.0 - weight_high)
    blended = jnp.where(level < BUF, low, jnp.where(level >= grid[0] - BUF, high, own))
    root = jnp.exp(jnp.log(blended + 1e-06) * (1.0 / 3.0))
    new_grid = external[...] - xc_factor * root
    grid_ref[...] = new_grid
    cosv = jnp.cos(half_step * new_grid)
    sinv = jnp.sin(half_step * new_grid)
    for plane in range(slab):
        low_row = plane * cells
        real = field[low_row : low_row + cells]
        imag = field[half + low_row : half + low_row + cells]
        cos_b = spread_column(cosv[plane : plane + 1])
        sin_b = spread_column(sinv[plane : plane + 1])
        evolved_ref[low_row : low_row + cells] = (cos_b * real + sin_b * imag).astype(jnp.bfloat16)
        evolved_ref[half + low_row : half + low_row + cells] = (
            cos_b * imag - sin_b * real
        ).astype(jnp.bfloat16)


def contract(left, right):
    return lax.dot_general(
        left, right, (((0,), (0,)), ((), ())), preferred_element_type=jnp.float32
    )


def high_dot(left, right):
    return jnp.dot(
        left, right, precision=lax.Precision.HIGHEST, preferred_element_type=jnp.float32
    )


def half_dot(left, right):
    return jnp.dot(left, right, preferred_element_type=jnp.float32)


def pieces(value):
    high = lax.reduce_precision(value, 8, 7)
    rest = value - high
    middle = lax.reduce_precision(rest, 8, 7)
    low = rest - middle
    rows = value.shape[0]
    pad = jnp.zeros((8 - rows,) + value.shape[1:], value.dtype)
    stacked = jnp.concatenate([high, pad, middle, pad, low, pad, jnp.zeros((8,) + value.shape[1:])])
    return stacked.astype(jnp.bfloat16)


def scalars(count):
    return [pl.BlockSpec(memory_space=pltpu.SMEM)] + [
        pl.BlockSpec(memory_space=pltpu.VMEM) for _ in range(count)
    ]


def shards(orbitals, initial, potential, external, occupation, coupling, neighbours, offsets):
    slab, rows_y, cols_z, orbits = initial.shape[2:]
    grid = (rows_y, cols_z)
    cells = rows_y * cols_z
    rows = 2 * slab * cells
    start = initial.reshape(rows, orbits)
    devices = lax.axis_size("space")
    place = lax.axis_index("space")
    f32, bf16 = jnp.float32, jnp.bfloat16
    edge = jnp.stack([place > 0, place < devices - 1]).astype(f32)
    planes = (2, 3 * slab) + grid + (orbits,)
    stencil = [pltpu.VMEM(planes, f32) for _ in range(3)]
    orbs = orbitals.reshape(rows, orbits)
    message = jnp.concatenate([start, orbs, pieces(potential[0])])
    low_m, high_m = neighbour_pair(message, "space")
    scale = 1.0 / (slab * devices * cells)
    shape = jax.ShapeDtypeStruct
    partial, moved, sent, turned = pl.pallas_call(
        lambda *refs: front_kernel(slab, grid, scale, *refs),
        out_shape=(
            shape((6 * orbits, orbits), bf16),
            shape((rows, orbits), bf16),
            shape((rows, orbits), bf16),
            shape((rows, orbits), f32),
        ),
        in_specs=scalars(4),
        scratch_shapes=stencil
        + [pltpu.VMEM((3 * slab, cells, orbits), f32) for _ in range(2)]
        + [
            pltpu.VMEM((2, slab, cells, orbits), f32),
            pltpu.VMEM((rows, orbits), bf16),
            pltpu.VMEM((rows, 4 * orbits), bf16),
        ],
        compiler_params=pltpu.CompilerParams(vmem_limit_bytes=20 << 20),
        name="front",
    )(edge, low_m, message, high_m, potential[0])

    share = 6 * orbits // devices
    parts = lax.all_to_all(partial.reshape(devices, share, orbits), "space", 0, 0, tiled=True)
    low_s, high_s = neighbour_pair(sent, "space")
    spread = pl.pallas_call(
        sum_kernel,
        out_shape=shape((devices, share, orbits), bf16),
        compiler_params=pltpu.CompilerParams(vmem_limit_bytes=6 << 20),
        name="total",
    )(parts)
    sums = lax.all_to_all(spread, "space", 0, 0, tiled=True).reshape(6 * orbits, orbits)
    second = pl.pallas_call(
        lambda *refs: second_kernel(slab, grid, *refs),
        out_shape=shape((rows, orbits), f32),
        in_specs=scalars(5),
        scratch_shapes=stencil + [pltpu.VMEM((slab, cells, orbits), f32) for _ in range(2)],
        compiler_params=pltpu.CompilerParams(vmem_limit_bytes=14 << 20),
        name="second",
    )(edge, low_s, sent, high_s, turned, potential[0])

    domain_count = neighbours.shape[0]
    intersection, field, density = pl.pallas_call(
        lambda *refs: back_kernel(slab, *refs),
        out_shape=(
            shape((2 * orbits, orbits), f32),
            shape((rows, orbits), f32),
            shape((domain_count, slab, cells), f32),
        ),
        compiler_params=pltpu.CompilerParams(vmem_limit_bytes=14 << 20),
        name="back",
    )(sums, coupling, moved, start, second, occupation.reshape(1, orbits))
    gathered = lax.all_to_all(density, "dom", 0, 0, tiled=True)
    own_index = lax.axis_index("dom")
    mine = lax.dynamic_index_in_dim(neighbours, own_index, 0, keepdims=False)
    shift = lax.dynamic_index_in_dim(offsets, own_index, 0, keepdims=False)
    where = jnp.concatenate([mine, shift, own_index.reshape(1).astype(jnp.int32)])
    new_grid, evolved = pl.pallas_call(
        lambda *refs: tail_kernel(slab, grid, *refs),
        out_shape=(shape((slab, cells), f32), shape((rows, orbits), bf16)),
        in_specs=scalars(3),
        compiler_params=pltpu.CompilerParams(vmem_limit_bytes=8 << 20),
        name="tail",
    )(where, gathered, external[0], field)
    return (
        evolved.reshape(orbitals.shape),
        intersection.reshape(1, 2, orbits, orbits),
        new_grid[None],
    )


def solution(mesh):
    return jax.shard_map(
        shards,
        mesh=mesh,
        in_specs=(
            P("dom", None, "space", None, None, None),
            P("dom", None, "space", None, None, None),
            P("dom", "space", None),
            P("dom", "space", None),
            P(),
            P(),
            P(),
            P(),
        ),
        out_specs=(
            P("dom", None, "space", None, None, None),
            P("dom", None, None, None),
            P("dom", "space", None),
        ),
        check_vma=False,
    )
```

```python
import jax
import jax.numpy as jnp
from jax import lax
from jax.experimental import pallas as pl
from jax.experimental.pallas import tpu as pltpu
from jax.sharding import PartitionSpec as P


TAYLOR = 4
BUF = 4

time_step = 0.4
half_step = 0.2
xc_factor = 0.9847450218426965


def neighbour_pair(value, axis):
    devices = lax.axis_size(axis)
    up = [(i, i + 1) for i in range(devices - 1)]
    down = [(i + 1, i) for i in range(devices - 1)]
    return lax.ppermute(value, axis, up), lax.ppermute(value, axis, down)


def rounded(value):
    return value.astype(jnp.bfloat16).astype(jnp.float32)


def spread_column(row):
    return jnp.broadcast_to(row, (row.shape[-1], row.shape[-1])).T


def laplace(ref, part, plane):
    center = ref[part, plane]
    side = center.shape[1]
    zero = jnp.zeros((1,) + center.shape[1:], jnp.float32)
    total = ref[part, plane - 1] + ref[part, plane + 1]
    total = total + jnp.concatenate([center[1:], zero]) + jnp.concatenate([zero, center[:-1]])
    level = lax.broadcasted_iota(jnp.int32, center.shape, 1)
    total = total + jnp.where(level == side - 1, 0.0, pltpu.roll(center, side - 1, 1))
    total = total + jnp.where(level == 0, 0.0, pltpu.roll(center, 1, 1))
    return total - 6.0 * center


def kinetic(edge, running, even, odd, slab, grid, exact):
    planes = 3 * slab
    cells = grid[0] * grid[1]
    now, after = even, odd
    for order in range(1, TAYLOR + 1):
        factor = time_step / (2.0 * order)
        spans = ((order, slab, 0), (slab, 2 * slab, None), (2 * slab, planes - order, 1))
        for begin, end, side in spans:
            keep = factor if side is None else edge[side] * factor

            def one(plane, carry, now=now, after=after, keep=keep, side=side, order=order):
                real = -keep * laplace(now, 1, plane)
                imag = keep * laplace(now, 0, plane)
                for part, update in enumerate((real, imag)):
                    if side is None:
                        running[part, plane - slab] = running[part, plane - slab] + update
                    if order < TAYLOR:
                        if not exact:
                            flat = update.reshape(cells, update.shape[-1])
                            update = rounded(flat).reshape(update.shape)
                        after[part, plane] = update
                return carry

            if begin < end:
                lax.fori_loop(begin, end, one, 0)
        now, after = after, now


def fill_phase(potential, row, place, cos_ref, sin_ref, slab):
    cosv = jnp.cos(half_step * potential)
    sinv = jnp.sin(half_step * potential)
    for plane in range(slab):
        cos_ref[place + plane] = spread_column(cosv[row + plane : row + plane + 1])
        sin_ref[place + plane] = spread_column(sinv[row + plane : row + plane + 1])


def start_kernel(slab, grid, scale, edge, low_ref, own_ref, high_ref, field_ref, pot,
                 partial_ref, moved_ref, adjoint_ref, cos_ref, sin_ref,
                 even, odd, running, part_ref, right):
    cells = grid[0] * grid[1]
    half = slab * cells
    lanes = own_ref.shape[-1]
    tail = 2 * half
    box = grid + (lanes,)
    for group, ref in ((0, low_ref), (2, high_ref)):
        extra = ref[tail : tail + 32].astype(jnp.float32)
        whole = extra[0:8] + extra[8:16] + extra[16:24]
        fill_phase(whole, 0, group * slab, cos_ref, sin_ref, slab)
    fill_phase(pot[...], 0, slab, cos_ref, sin_ref, slab)

    for part in range(2):
        for group, ref in enumerate((low_ref, own_ref, high_ref)):

            def begin(plane, carry, ref=ref, group=group, part=part):
                rows = pl.multiple_of((part * slab + plane) * cells, cells)
                value = ref[pl.ds(rows, cells), :].astype(jnp.float32)
                at = group * slab + plane
                real = (cos_ref[at] * value).reshape(box)
                imag = (-sin_ref[at] * value).reshape(box)
                even[0, at] = real
                even[1, at] = imag
                if group == 1:
                    running[0, plane] = real
                    running[1, plane] = imag
                return carry

            lax.fori_loop(0, slab, begin, 0)
        kinetic(edge, running, even, odd, slab, grid, True)
        for plane in range(slab):
            real, imag = turned_back(running, plane, cos_ref, sin_ref, slab)
            low = slice(plane * cells, (plane + 1) * cells)
            high = slice(half + plane * cells, half + (plane + 1) * cells)
            if part == 0:
                part_ref[0, plane] = real
                part_ref[1, plane] = imag
            else:
                kept_real = part_ref[0, plane]
                kept_imag = part_ref[1, plane]
                moved_ref[low] = (kept_real - imag).astype(jnp.bfloat16)
                moved_ref[high] = (kept_imag + real).astype(jnp.bfloat16)
                adjoint_ref[low] = (kept_real + imag).astype(jnp.bfloat16)
                adjoint_ref[high] = (real - kept_imag).astype(jnp.bfloat16)
    for place, ref in ((0, field_ref), (2, own_ref)):
        right[:half, place * lanes : (place + 1) * lanes] = ref[:half]
        right[half:, place * lanes : (place + 1) * lanes] = ref[half : 2 * half]
        right[:half, (place + 1) * lanes : (place + 2) * lanes] = ref[half : 2 * half]
        right[half:, (place + 1) * lanes : (place + 2) * lanes] = -ref[:half]
    over = contract(adjoint_ref[...], right[...]) * scale
    for index in range(4):
        piece = slice(index * lanes, (index + 1) * lanes)
        partial_ref[piece] = over[:, piece].astype(jnp.bfloat16)


def turned_back(running, plane, cos_ref, sin_ref, slab):
    shape = cos_ref.shape[1:]
    real = running[0, plane].reshape(shape)
    imag = running[1, plane].reshape(shape)
    cosv = cos_ref[slab + plane]
    sinv = sin_ref[slab + plane]
    return cosv * real + sinv * imag, cosv * imag - sinv * real


def first_kernel(slab, grid, scale, edge, low_ref, own_ref, high_ref, adjoint, cos_ref, sin_ref,
                 partial_ref, sent_ref, turned_ref, even, odd, running, right):
    cells = grid[0] * grid[1]
    half = slab * cells
    lanes = own_ref.shape[-1]
    box = grid + (lanes,)
    for group, ref in enumerate((low_ref, own_ref, high_ref)):

        def begin(plane, carry, ref=ref, group=group):
            rows = pl.multiple_of(plane * cells, cells)
            real = ref[pl.ds(rows, cells), :].astype(jnp.float32)
            imag = ref[pl.ds(half + rows, cells), :].astype(jnp.float32)
            at = group * slab + plane
            cosv = cos_ref[at]
            sinv = sin_ref[at]
            for part, value in enumerate((cosv * real + sinv * imag, cosv * imag - sinv * real)):
                even[part, at] = rounded(value).reshape(box)
                if group == 1:
                    running[part, plane] = value.reshape(box)
            return carry

        lax.fori_loop(0, slab, begin, 0)
    kinetic(edge, running, even, odd, slab, grid, False)
    for plane in range(slab):
        real, imag = turned_back(running, plane, cos_ref, sin_ref, slab)
        low = slice(plane * cells, (plane + 1) * cells)
        high = slice(half + plane * cells, half + (plane + 1) * cells)
        cosv = cos_ref[slab + plane]
        sinv = sin_ref[slab + plane]
        turned_real = cosv * real + sinv * imag
        turned_imag = cosv * imag - sinv * real
        turned_ref[low] = turned_real
        turned_ref[high] = turned_imag
        sent_ref[low] = turned_real.astype(jnp.bfloat16)
        sent_ref[high] = turned_imag.astype(jnp.bfloat16)
        first_real = real.astype(jnp.bfloat16)
        first_imag = imag.astype(jnp.bfloat16)
        right[low, :lanes] = first_real
        right[low, lanes:] = first_imag
        right[high, :lanes] = first_imag
        right[high, lanes:] = -first_real
    cross = contract(adjoint[...], right[...]) * scale
    partial_ref[:lanes] = cross[:, :lanes].astype(jnp.bfloat16)
    partial_ref[lanes:] = cross[:, lanes:].astype(jnp.bfloat16)


def second_kernel(slab, grid, edge, low, own, high, turned, cos_ref, sin_ref, second_ref,
                  even, odd, running):
    cells = grid[0] * grid[1]
    half = slab * cells
    lanes = own.shape[-1]
    box = grid + (lanes,)
    for part in range(2):
        for group, ref in enumerate((low, own, high)):

            def begin(plane, carry, ref=ref, group=group, part=part):
                at = pl.multiple_of((part * slab + plane) * cells, cells)
                value = ref[pl.ds(at, cells), :].astype(jnp.float32).reshape(box)
                even[part, group * slab + plane] = value
                if group == 1:
                    running[part, plane] = turned[pl.ds(at, cells), :].reshape(box)
                return carry

            lax.fori_loop(0, slab, begin, 0)
    kinetic(edge, running, even, odd, slab, grid, False)
    for plane in range(slab):
        real, imag = turned_back(running, plane, cos_ref, sin_ref, slab)
        at = plane * cells
        second_ref[at : at + cells] = real
        second_ref[half + at : half + at + cells] = imag


def sum_kernel(main_ref, cross_ref, out_ref):
    split = main_ref.shape[1]
    for rows, ref in ((slice(0, split), main_ref), (slice(split, None), cross_ref)):
        total = ref[0].astype(jnp.float32)
        for index in range(1, ref.shape[0]):
            total = total + ref[index].astype(jnp.float32)
        total = total.astype(jnp.bfloat16)
        for index in range(out_ref.shape[0]):
            out_ref[index, rows] = total


def back_kernel(slab, gathered, coupling, moved, start, second, occupation,
                inter_ref, field_ref, density_ref):
    lanes = coupling.shape[-1]
    half = start.shape[0] // 2
    cells = half // slab
    strength = coupling[...]
    share = 4 * lanes // gathered.shape[0]
    sums = gathered[:, :share].astype(jnp.float32).reshape(4 * lanes, lanes)
    cross = gathered[:, share:].astype(jnp.float32).reshape(2 * lanes, lanes)

    def matrix(index):
        return sums[index * lanes : (index + 1) * lanes]

    def mixed(real, imag):
        return (
            high_dot(strength, real).astype(jnp.bfloat16),
            high_dot(strength, imag).astype(jnp.bfloat16),
        )

    mix1_real, mix1_imag = mixed(matrix(0), matrix(1))
    gram_real, gram_imag = matrix(2).astype(jnp.bfloat16), matrix(3).astype(jnp.bfloat16)
    over_real = cross[:lanes] + time_step * (
        half_dot(gram_real, mix1_imag) + half_dot(gram_imag, mix1_real)
    )
    over_imag = cross[lanes:] - time_step * (
        half_dot(gram_real, mix1_real) - half_dot(gram_imag, mix1_imag)
    )
    inter_ref[:lanes] = over_real
    inter_ref[lanes:] = over_imag
    mix2_real, mix2_imag = mixed(over_real, over_imag)
    mix1_real_imag = jnp.concatenate([mix1_real, mix1_imag], axis=1)
    mix1_turned = jnp.concatenate([-mix1_imag, mix1_real], axis=1)
    mix2_real_imag = jnp.concatenate([mix2_real, mix2_imag], axis=1)
    mix2_turned = jnp.concatenate([-mix2_imag, mix2_real], axis=1)
    weight = jnp.broadcast_to(occupation[...], (8, lanes))
    for plane in range(slab):
        low = plane * cells
        real_rows = slice(low, low + cells)
        imag_rows = slice(half + low, half + low + cells)
        corr = (
            half_dot(moved[real_rows], mix1_real_imag)
            + half_dot(moved[imag_rows], mix1_turned)
            + half_dot(start[real_rows], mix2_real_imag)
            + half_dot(start[imag_rows], mix2_turned)
        )
        real = second[real_rows] + time_step * corr[:, lanes:]
        imag = second[imag_rows] - time_step * corr[:, :lanes]
        field_ref[real_rows] = real
        field_ref[imag_rows] = imag
        square = real * real + imag * imag
        dense = lax.dot_general(
            weight,
            square,
            (((1,), (1,)), ((), ())),
            precision=lax.Precision.HIGHEST,
            preferred_element_type=jnp.float32,
        )
        for owner in range(density_ref.shape[0]):
            density_ref[owner, plane : plane + 1] = dense[:1]


def tail_kernel(slab, grid, place, gathered, external, field, grid_ref, evolved_ref):
    lanes = external.shape[-1]
    half = field.shape[0] // 2
    cells = half // slab
    side = grid[1]
    own = gathered[place[4]]
    lower = gathered[place[0]]
    upper = gathered[place[1]]
    lower = pltpu.roll(lower, (lanes - place[2] * side) % lanes, 1)
    upper = pltpu.roll(upper, (2 * lanes - BUF * side - place[3] * side) % lanes, 1)
    level = lax.broadcasted_iota(jnp.int32, own.shape, 1) // side
    step = level.astype(jnp.float32)
    weight_low = (step + 1.0) / (BUF + 1.0)
    weight_high = (grid[0] - step) / (BUF + 1.0)
    low = own * weight_low + lower * (1.0 - weight_low)
    high = own * weight_high + upper * (1.0 - weight_high)
    blended = jnp.where(level < BUF, low, jnp.where(level >= grid[0] - BUF, high, own))
    root = jnp.exp(jnp.log(blended + 1e-06) * (1.0 / 3.0))
    new_grid = external[...] - xc_factor * root
    grid_ref[...] = new_grid
    cosv = jnp.cos(half_step * new_grid)
    sinv = jnp.sin(half_step * new_grid)
    for plane in range(slab):
        low_row = plane * cells
        real = field[low_row : low_row + cells]
        imag = field[half + low_row : half + low_row + cells]
        cos_b = spread_column(cosv[plane : plane + 1])
        sin_b = spread_column(sinv[plane : plane + 1])
        evolved_ref[low_row : low_row + cells] = (cos_b * real + sin_b * imag).astype(jnp.bfloat16)
        evolved_ref[half + low_row : half + low_row + cells] = (
            cos_b * imag - sin_b * real
        ).astype(jnp.bfloat16)


def contract(left, right):
    return lax.dot_general(
        left, right, (((0,), (0,)), ((), ())), preferred_element_type=jnp.float32
    )


def high_dot(left, right):
    return jnp.dot(
        left, right, precision=lax.Precision.HIGHEST, preferred_element_type=jnp.float32
    )


def half_dot(left, right):
    return jnp.dot(left, right, preferred_element_type=jnp.float32)


def pieces(value):
    high = lax.reduce_precision(value, 8, 7)
    rest = value - high
    middle = lax.reduce_precision(rest, 8, 7)
    low = rest - middle
    rows = value.shape[0]
    pad = jnp.zeros((8 - rows,) + value.shape[1:], value.dtype)
    stacked = jnp.concatenate([high, pad, middle, pad, low, pad, jnp.zeros((8,) + value.shape[1:])])
    return stacked.astype(jnp.bfloat16)


def scalars(count):
    return [pl.BlockSpec(memory_space=pltpu.SMEM)] + [
        pl.BlockSpec(memory_space=pltpu.VMEM) for _ in range(count)
    ]


def shards(orbitals, initial, potential, external, occupation, coupling, neighbours, offsets):
    slab, rows_y, cols_z, orbits = initial.shape[2:]
    grid = (rows_y, cols_z)
    cells = rows_y * cols_z
    rows = 2 * slab * cells
    start = initial.reshape(rows, orbits)
    devices = lax.axis_size("space")
    place = lax.axis_index("space")
    f32, bf16 = jnp.float32, jnp.bfloat16
    edge = jnp.stack([place > 0, place < devices - 1]).astype(f32)
    planes = (2, 3 * slab) + grid + (orbits,)
    stencil = [pltpu.VMEM(planes, f32), pltpu.VMEM(planes, f32)]
    stencil = stencil + [pltpu.VMEM((2, slab) + grid + (orbits,), f32)]
    shape = jax.ShapeDtypeStruct
    orbs = orbitals.reshape(rows, orbits)
    message = jnp.concatenate([start, pieces(potential[0])])
    low_m, high_m = neighbour_pair(message, "space")
    low_o, high_o = neighbour_pair(orbs, "space")
    scale = 1.0 / (slab * devices * cells)
    turn = shape((3 * slab, cells, orbits), f32)

    def limit(mib):
        return pltpu.CompilerParams(vmem_limit_bytes=mib << 20)

    def shared(value):
        share = value.shape[0] // devices
        parts = lax.all_to_all(
            value.reshape(devices, share, orbits), "space", 0, 0, tiled=True
        )
        return parts

    partial, moved, adjoint, cosv, sinv = pl.pallas_call(
        lambda *refs: start_kernel(slab, grid, scale, *refs),
        out_shape=(
            shape((4 * orbits, orbits), bf16),
            shape((rows, orbits), bf16),
            shape((rows, orbits), bf16),
            turn,
            turn,
        ),
        in_specs=scalars(5),
        scratch_shapes=stencil
        + [
            pltpu.VMEM((2, slab, cells, orbits), f32),
            pltpu.VMEM((rows, 4 * orbits), bf16),
        ],
        compiler_params=limit(16),
        name="start",
    )(edge, low_m, start, high_m, orbs, potential[0])
    parts = shared(partial)
    partial, sent, turned = pl.pallas_call(
        lambda *refs: first_kernel(slab, grid, scale, *refs),
        out_shape=(
            shape((2 * orbits, orbits), bf16),
            shape((rows, orbits), bf16),
            shape((rows, orbits), f32),
        ),
        in_specs=scalars(6),
        scratch_shapes=stencil + [pltpu.VMEM((rows, 2 * orbits), bf16)],
        compiler_params=limit(14),
        name="first",
    )(edge, low_o, orbs, high_o, adjoint, cosv, sinv)
    cross_parts = shared(partial)
    low_s, high_s = neighbour_pair(sent, "space")
    spread = pl.pallas_call(
        sum_kernel,
        out_shape=shape((devices, 6 * orbits // devices, orbits), bf16),
        compiler_params=limit(6),
        name="total",
    )(parts, cross_parts)
    sums = lax.all_to_all(spread, "space", 0, 0, tiled=True)
    second = pl.pallas_call(
        lambda *refs: second_kernel(slab, grid, *refs),
        out_shape=shape((rows, orbits), f32),
        in_specs=scalars(6),
        scratch_shapes=stencil,
        compiler_params=limit(12),
        name="second",
    )(edge, low_s, sent, high_s, turned, cosv, sinv)

    domain_count = neighbours.shape[0]
    intersection, field, density = pl.pallas_call(
        lambda *refs: back_kernel(slab, *refs),
        out_shape=(
            shape((2 * orbits, orbits), f32),
            shape((rows, orbits), f32),
            shape((domain_count, slab, cells), f32),
        ),
        compiler_params=limit(14),
        name="back",
    )(sums, coupling, moved, start, second, occupation.reshape(1, orbits))
    gathered = lax.all_to_all(density, "dom", 0, 0, tiled=True)
    own_index = lax.axis_index("dom")
    mine = lax.dynamic_index_in_dim(neighbours, own_index, 0, keepdims=False)
    shift = lax.dynamic_index_in_dim(offsets, own_index, 0, keepdims=False)
    where = jnp.concatenate([mine, shift, own_index.reshape(1).astype(jnp.int32)])
    new_grid, evolved = pl.pallas_call(
        lambda *refs: tail_kernel(slab, grid, *refs),
        out_shape=(shape((slab, cells), f32), shape((rows, orbits), bf16)),
        in_specs=scalars(3),
        compiler_params=limit(8),
        name="tail",
    )(where, gathered, external[0], field)
    return (
        evolved.reshape(orbitals.shape),
        intersection.reshape(1, 2, orbits, orbits),
        new_grid[None],
    )


def solution(mesh):
    return jax.shard_map(
        shards,
        mesh=mesh,
        in_specs=(
            P("dom", None, "space", None, None, None),
            P("dom", None, "space", None, None, None),
            P("dom", "space", None),
            P("dom", "space", None),
            P(),
            P(),
            P(),
            P(),
        ),
        out_specs=(
            P("dom", None, "space", None, None, None),
            P("dom", None, None, None),
            P("dom", "space", None),
        ),
        check_vma=False,
    )
```

```python
import jax
import jax.numpy as jnp
from jax import lax
from jax.experimental import pallas as pl
from jax.experimental.pallas import tpu as pltpu
from jax.sharding import PartitionSpec as P


TAYLOR = 4
BUF = 4

time_step = 0.4
half_step = 0.2
xc_factor = 0.9847450218426965


def neighbour_pair(value, axis):
    devices = lax.axis_size(axis)
    up = [(i, i + 1) for i in range(devices - 1)]
    down = [(i + 1, i) for i in range(devices - 1)]
    return lax.ppermute(value, axis, up), lax.ppermute(value, axis, down)


def rounded(value):
    return value.astype(jnp.bfloat16).astype(jnp.float32)


def spread_column(row):
    return jnp.broadcast_to(row, (row.shape[-1], row.shape[-1])).T


def laplace(ref, part, plane):
    center = ref[part, plane]
    side = center.shape[1]
    zero = jnp.zeros((1,) + center.shape[1:], jnp.float32)
    total = ref[part, plane - 1] + ref[part, plane + 1]
    total = total + jnp.concatenate([center[1:], zero]) + jnp.concatenate([zero, center[:-1]])
    level = lax.broadcasted_iota(jnp.int32, center.shape, 1)
    total = total + jnp.where(level == side - 1, 0.0, pltpu.roll(center, side - 1, 1))
    total = total + jnp.where(level == 0, 0.0, pltpu.roll(center, 1, 1))
    return total - 6.0 * center


def kinetic(edge, running, even, odd, slab, grid, exact):
    planes = 3 * slab
    cells = grid[0] * grid[1]
    now, after = even, odd
    for order in range(1, TAYLOR + 1):
        factor = time_step / (2.0 * order)
        spans = ((order, slab, 0), (slab, 2 * slab, None), (2 * slab, planes - order, 1))
        for begin, end, side in spans:
            keep = factor if side is None else edge[side] * factor

            def one(plane, carry, now=now, after=after, keep=keep, side=side, order=order):
                real = -keep * laplace(now, 1, plane)
                imag = keep * laplace(now, 0, plane)
                for part, update in enumerate((real, imag)):
                    if side is None:
                        running[part, plane - slab] = running[part, plane - slab] + update
                    if order < TAYLOR:
                        if not exact:
                            flat = update.reshape(cells, update.shape[-1])
                            update = rounded(flat).reshape(update.shape)
                        after[part, plane] = update
                return carry

            if begin < end:
                lax.fori_loop(begin, end, one, 0)
        now, after = after, now


def fill_phase(potential, row, place, cos_ref, sin_ref, slab):
    cosv = jnp.cos(half_step * potential)
    sinv = jnp.sin(half_step * potential)
    for plane in range(slab):
        cos_ref[place + plane] = spread_column(cosv[row + plane : row + plane + 1])
        sin_ref[place + plane] = spread_column(sinv[row + plane : row + plane + 1])


def start_kernel(slab, grid, scale, edge, low_ref, own_ref, high_ref, field_ref, pot,
                 partial_ref, moved_ref, adjoint_ref, cos_ref, sin_ref,
                 even, odd, running, part_ref, right):
    cells = grid[0] * grid[1]
    half = slab * cells
    lanes = own_ref.shape[-1]
    tail = 2 * half
    box = grid + (lanes,)
    for group, ref in ((0, low_ref), (2, high_ref)):
        extra = ref[tail : tail + 32].astype(jnp.float32)
        whole = extra[0:8] + extra[8:16] + extra[16:24]
        fill_phase(whole, 0, group * slab, cos_ref, sin_ref, slab)
    fill_phase(pot[...], 0, slab, cos_ref, sin_ref, slab)

    for part in range(2):
        for group, ref in enumerate((low_ref, own_ref, high_ref)):

            def begin(plane, carry, ref=ref, group=group, part=part):
                rows = pl.multiple_of((part * slab + plane) * cells, cells)
                value = ref[pl.ds(rows, cells), :].astype(jnp.float32)
                at = group * slab + plane
                real = (cos_ref[at] * value).reshape(box)
                imag = (-sin_ref[at] * value).reshape(box)
                even[0, at] = real
                even[1, at] = imag
                if group == 1:
                    running[0, plane] = real
                    running[1, plane] = imag
                return carry

            lax.fori_loop(0, slab, begin, 0)
        kinetic(edge, running, even, odd, slab, grid, True)
        for plane in range(slab):
            real, imag = turned_back(running, plane, cos_ref, sin_ref, slab)
            low = slice(plane * cells, (plane + 1) * cells)
            high = slice(half + plane * cells, half + (plane + 1) * cells)
            if part == 0:
                part_ref[0, plane] = real
                part_ref[1, plane] = imag
            else:
                kept_real = part_ref[0, plane]
                kept_imag = part_ref[1, plane]
                moved_ref[low] = (kept_real - imag).astype(jnp.bfloat16)
                moved_ref[high] = (kept_imag + real).astype(jnp.bfloat16)
                adjoint_ref[low] = (kept_real + imag).astype(jnp.bfloat16)
                adjoint_ref[high] = (real - kept_imag).astype(jnp.bfloat16)
    for place, ref in ((0, field_ref), (2, own_ref)):
        right[:half, place * lanes : (place + 1) * lanes] = ref[:half]
        right[half:, place * lanes : (place + 1) * lanes] = ref[half : 2 * half]
        right[:half, (place + 1) * lanes : (place + 2) * lanes] = ref[half : 2 * half]
        right[half:, (place + 1) * lanes : (place + 2) * lanes] = -ref[:half]
    over = contract(adjoint_ref[...], right[...]) * scale
    for index in range(4):
        piece = slice(index * lanes, (index + 1) * lanes)
        partial_ref[piece] = over[:, piece].astype(jnp.bfloat16)


def turned_back(running, plane, cos_ref, sin_ref, slab):
    shape = cos_ref.shape[1:]
    real = running[0, plane].reshape(shape)
    imag = running[1, plane].reshape(shape)
    cosv = cos_ref[slab + plane]
    sinv = sin_ref[slab + plane]
    return cosv * real + sinv * imag, cosv * imag - sinv * real


def first_kernel(slab, grid, scale, edge, low_ref, own_ref, high_ref, adjoint, cos_ref, sin_ref, over,
                 partial_ref, sent_ref, turned_ref, even, odd, running, right):
    cells = grid[0] * grid[1]
    half = slab * cells
    lanes = own_ref.shape[-1]
    box = grid + (lanes,)
    for group, ref in enumerate((low_ref, own_ref, high_ref)):

        def begin(plane, carry, ref=ref, group=group):
            rows = pl.multiple_of(plane * cells, cells)
            real = ref[pl.ds(rows, cells), :].astype(jnp.float32)
            imag = ref[pl.ds(half + rows, cells), :].astype(jnp.float32)
            at = group * slab + plane
            cosv = cos_ref[at]
            sinv = sin_ref[at]
            for part, value in enumerate((cosv * real + sinv * imag, cosv * imag - sinv * real)):
                even[part, at] = rounded(value).reshape(box)
                if group == 1:
                    running[part, plane] = value.reshape(box)
            return carry

        lax.fori_loop(0, slab, begin, 0)
    kinetic(edge, running, even, odd, slab, grid, False)
    for plane in range(slab):
        real, imag = turned_back(running, plane, cos_ref, sin_ref, slab)
        low = slice(plane * cells, (plane + 1) * cells)
        high = slice(half + plane * cells, half + (plane + 1) * cells)
        cosv = cos_ref[slab + plane]
        sinv = sin_ref[slab + plane]
        turned_real = cosv * real + sinv * imag
        turned_imag = cosv * imag - sinv * real
        turned_ref[low] = turned_real
        turned_ref[high] = turned_imag
        sent_ref[low] = turned_real.astype(jnp.bfloat16)
        sent_ref[high] = turned_imag.astype(jnp.bfloat16)
        first_real = real.astype(jnp.bfloat16)
        first_imag = imag.astype(jnp.bfloat16)
        right[low, :lanes] = first_real
        right[low, lanes:] = first_imag
        right[high, :lanes] = first_imag
        right[high, lanes:] = -first_real
    cross = contract(adjoint[...], right[...]) * scale
    partial_ref[: 2 * lanes] = over[: 2 * lanes]
    partial_ref[2 * lanes : 3 * lanes] = cross[:, :lanes].astype(jnp.bfloat16)
    partial_ref[3 * lanes : 4 * lanes] = cross[:, lanes:].astype(jnp.bfloat16)
    partial_ref[4 * lanes :] = over[2 * lanes :]


def second_kernel(slab, grid, edge, low, own, high, turned, cos_ref, sin_ref, second_ref,
                  even, odd, running):
    cells = grid[0] * grid[1]
    half = slab * cells
    lanes = own.shape[-1]
    box = grid + (lanes,)
    for part in range(2):
        for group, ref in enumerate((low, own, high)):

            def begin(plane, carry, ref=ref, group=group, part=part):
                at = pl.multiple_of((part * slab + plane) * cells, cells)
                value = ref[pl.ds(at, cells), :].astype(jnp.float32).reshape(box)
                even[part, group * slab + plane] = value
                if group == 1:
                    running[part, plane] = turned[pl.ds(at, cells), :].reshape(box)
                return carry

            lax.fori_loop(0, slab, begin, 0)
    kinetic(edge, running, even, odd, slab, grid, False)
    for plane in range(slab):
        real, imag = turned_back(running, plane, cos_ref, sin_ref, slab)
        at = plane * cells
        second_ref[at : at + cells] = real
        second_ref[half + at : half + at + cells] = imag


def sum_kernel(parts_ref, out_ref):
    total = parts_ref[0].astype(jnp.float32)
    for index in range(1, parts_ref.shape[0]):
        total = total + parts_ref[index].astype(jnp.float32)
    total = total.astype(jnp.bfloat16)
    for index in range(out_ref.shape[0]):
        out_ref[index] = total


def back_kernel(slab, sums, coupling, moved, start, second, occupation,
                inter_ref, field_ref, density_ref):
    lanes = coupling.shape[-1]
    half = start.shape[0] // 2
    cells = half // slab
    strength = coupling[...]

    def matrix(index):
        return sums[index * lanes : (index + 1) * lanes]

    def mixed(real, imag):
        return (
            high_dot(strength, real).astype(jnp.bfloat16),
            high_dot(strength, imag).astype(jnp.bfloat16),
        )

    mix1_real, mix1_imag = mixed(
        matrix(0).astype(jnp.float32), matrix(1).astype(jnp.float32)
    )
    gram_real, gram_imag = matrix(4), matrix(5)
    over_real = matrix(2).astype(jnp.float32) + time_step * (
        half_dot(gram_real, mix1_imag) + half_dot(gram_imag, mix1_real)
    )
    over_imag = matrix(3).astype(jnp.float32) - time_step * (
        half_dot(gram_real, mix1_real) - half_dot(gram_imag, mix1_imag)
    )
    inter_ref[:lanes] = over_real
    inter_ref[lanes:] = over_imag
    mix2_real, mix2_imag = mixed(over_real, over_imag)
    mix1_real_imag = jnp.concatenate([mix1_real, mix1_imag], axis=1)
    mix1_turned = jnp.concatenate([-mix1_imag, mix1_real], axis=1)
    mix2_real_imag = jnp.concatenate([mix2_real, mix2_imag], axis=1)
    mix2_turned = jnp.concatenate([-mix2_imag, mix2_real], axis=1)
    weight = jnp.broadcast_to(occupation[...], (8, lanes))
    for plane in range(slab):
        low = plane * cells
        real_rows = slice(low, low + cells)
        imag_rows = slice(half + low, half + low + cells)
        corr = (
            half_dot(moved[real_rows], mix1_real_imag)
            + half_dot(moved[imag_rows], mix1_turned)
            + half_dot(start[real_rows], mix2_real_imag)
            + half_dot(start[imag_rows], mix2_turned)
        )
        real = second[real_rows] + time_step * corr[:, lanes:]
        imag = second[imag_rows] - time_step * corr[:, :lanes]
        field_ref[real_rows] = real
        field_ref[imag_rows] = imag
        square = real * real + imag * imag
        dense = lax.dot_general(
            weight,
            square,
            (((1,), (1,)), ((), ())),
            precision=lax.Precision.HIGHEST,
            preferred_element_type=jnp.float32,
        )
        for owner in range(density_ref.shape[0]):
            density_ref[owner, plane : plane + 1] = dense[:1]


def tail_kernel(slab, grid, place, gathered, external, field, grid_ref, evolved_ref):
    lanes = external.shape[-1]
    half = field.shape[0] // 2
    cells = half // slab
    side = grid[1]
    own = gathered[place[4]]
    lower = gathered[place[0]]
    upper = gathered[place[1]]
    lower = pltpu.roll(lower, (lanes - place[2] * side) % lanes, 1)
    upper = pltpu.roll(upper, (2 * lanes - BUF * side - place[3] * side) % lanes, 1)
    level = lax.broadcasted_iota(jnp.int32, own.shape, 1) // side
    step = level.astype(jnp.float32)
    weight_low = (step + 1.0) / (BUF + 1.0)
    weight_high = (grid[0] - step) / (BUF + 1.0)
    low = own * weight_low + lower * (1.0 - weight_low)
    high = own * weight_high + upper * (1.0 - weight_high)
    blended = jnp.where(level < BUF, low, jnp.where(level >= grid[0] - BUF, high, own))
    root = jnp.exp(jnp.log(blended + 1e-06) * (1.0 / 3.0))
    new_grid = external[...] - xc_factor * root
    grid_ref[...] = new_grid
    cosv = jnp.cos(half_step * new_grid)
    sinv = jnp.sin(half_step * new_grid)
    for plane in range(slab):
        low_row = plane * cells
        real = field[low_row : low_row + cells]
        imag = field[half + low_row : half + low_row + cells]
        cos_b = spread_column(cosv[plane : plane + 1])
        sin_b = spread_column(sinv[plane : plane + 1])
        evolved_ref[low_row : low_row + cells] = (cos_b * real + sin_b * imag).astype(jnp.bfloat16)
        evolved_ref[half + low_row : half + low_row + cells] = (
            cos_b * imag - sin_b * real
        ).astype(jnp.bfloat16)


def contract(left, right):
    return lax.dot_general(
        left, right, (((0,), (0,)), ((), ())), preferred_element_type=jnp.float32
    )


def high_dot(left, right):
    return jnp.dot(
        left, right, precision=lax.Precision.HIGHEST, preferred_element_type=jnp.float32
    )


def half_dot(left, right):
    return jnp.dot(left, right, preferred_element_type=jnp.float32)


def pack_kernel(start_ref, pot, out_ref):
    rows = start_ref.shape[0]
    value = pot[...]
    high = rounded(value)
    middle = rounded(value - high)
    low = value - high - middle
    pad = jnp.zeros((8 - value.shape[0], value.shape[1]), value.dtype)
    none = jnp.zeros((8, value.shape[1]), value.dtype)
    out_ref[:rows] = start_ref[...]
    out_ref[rows:] = jnp.concatenate([high, pad, middle, pad, low, pad, none]).astype(jnp.bfloat16)


def scalars(count):
    return [pl.BlockSpec(memory_space=pltpu.SMEM)] + [
        pl.BlockSpec(memory_space=pltpu.VMEM) for _ in range(count)
    ]


def shards(orbitals, initial, potential, external, occupation, coupling, neighbours, offsets):
    slab, rows_y, cols_z, orbits = initial.shape[2:]
    grid = (rows_y, cols_z)
    cells = rows_y * cols_z
    rows = 2 * slab * cells
    start = initial.reshape(rows, orbits)
    devices = lax.axis_size("space")
    place = lax.axis_index("space")
    f32, bf16 = jnp.float32, jnp.bfloat16
    edge = jnp.stack([place > 0, place < devices - 1]).astype(f32)
    planes = (2, 3 * slab) + grid + (orbits,)
    stencil = [pltpu.VMEM(planes, f32), pltpu.VMEM(planes, f32)]
    stencil = stencil + [pltpu.VMEM((2, slab) + grid + (orbits,), f32)]
    shape = jax.ShapeDtypeStruct
    orbs = orbitals.reshape(rows, orbits)
    message = pl.pallas_call(
        pack_kernel,
        out_shape=shape((rows + 32, orbits), bf16),
        compiler_params=pltpu.CompilerParams(vmem_limit_bytes=3 << 20),
        name="pack",
    )(start, potential[0])
    low_m, high_m = neighbour_pair(message, "space")
    low_o, high_o = neighbour_pair(orbs, "space")
    scale = 1.0 / (slab * devices * cells)
    turn = shape((3 * slab, cells, orbits), f32)

    def limit(mib):
        return pltpu.CompilerParams(vmem_limit_bytes=mib << 20)

    over, moved, adjoint, cosv, sinv = pl.pallas_call(
        lambda *refs: start_kernel(slab, grid, scale, *refs),
        out_shape=(
            shape((4 * orbits, orbits), bf16),
            shape((rows, orbits), bf16),
            shape((rows, orbits), bf16),
            turn,
            turn,
        ),
        in_specs=scalars(5),
        scratch_shapes=stencil
        + [
            pltpu.VMEM((2, slab, cells, orbits), f32),
            pltpu.VMEM((rows, 4 * orbits), bf16),
        ],
        compiler_params=limit(16),
        name="start",
    )(edge, low_m, message, high_m, orbs, potential[0])
    partial, sent, turned = pl.pallas_call(
        lambda *refs: first_kernel(slab, grid, scale, *refs),
        out_shape=(
            shape((6 * orbits, orbits), bf16),
            shape((rows, orbits), bf16),
            shape((rows, orbits), f32),
        ),
        in_specs=scalars(7),
        scratch_shapes=stencil + [pltpu.VMEM((rows, 2 * orbits), bf16)],
        compiler_params=limit(14),
        name="first",
    )(edge, low_o, orbs, high_o, adjoint, cosv, sinv, over)
    share = 6 * orbits // devices
    parts = lax.all_to_all(partial.reshape(devices, share, orbits), "space", 0, 0, tiled=True)
    low_s, high_s = neighbour_pair(sent, "space")
    spread = pl.pallas_call(
        sum_kernel,
        out_shape=shape((devices, share, orbits), bf16),
        compiler_params=limit(6),
        name="total",
    )(parts)
    sums = lax.all_to_all(spread, "space", 0, 0, tiled=True)
    sums = sums.reshape(6 * orbits, orbits)
    second = pl.pallas_call(
        lambda *refs: second_kernel(slab, grid, *refs),
        out_shape=shape((rows, orbits), f32),
        in_specs=scalars(6),
        scratch_shapes=stencil,
        compiler_params=limit(12),
        name="second",
    )(edge, low_s, sent, high_s, turned, cosv, sinv)

    domain_count = neighbours.shape[0]
    intersection, field, density = pl.pallas_call(
        lambda *refs: back_kernel(slab, *refs),
        out_shape=(
            shape((2 * orbits, orbits), f32),
            shape((rows, orbits), f32),
            shape((domain_count, slab, cells), f32),
        ),
        compiler_params=limit(14),
        name="back",
    )(sums, coupling, moved, start, second, occupation.reshape(1, orbits))
    gathered = lax.all_to_all(density, "dom", 0, 0, tiled=True)
    own_index = lax.axis_index("dom")
    mine = lax.dynamic_index_in_dim(neighbours, own_index, 0, keepdims=False)
    shift = lax.dynamic_index_in_dim(offsets, own_index, 0, keepdims=False)
    where = jnp.concatenate([mine, shift, own_index.reshape(1).astype(jnp.int32)])
    new_grid, evolved = pl.pallas_call(
        lambda *refs: tail_kernel(slab, grid, *refs),
        out_shape=(shape((slab, cells), f32), shape((rows, orbits), bf16)),
        in_specs=scalars(3),
        compiler_params=limit(8),
        name="tail",
    )(where, gathered, external[0], field)
    return (
        evolved.reshape(orbitals.shape),
        intersection.reshape(1, 2, orbits, orbits),
        new_grid[None],
    )


def solution(mesh):
    return jax.shard_map(
        shards,
        mesh=mesh,
        in_specs=(
            P("dom", None, "space", None, None, None),
            P("dom", None, "space", None, None, None),
            P("dom", "space", None),
            P("dom", "space", None),
            P(),
            P(),
            P(),
            P(),
        ),
        out_specs=(
            P("dom", None, "space", None, None, None),
            P("dom", None, None, None),
            P("dom", "space", None),
        ),
        check_vma=False,
    )
```

```python
import jax
import jax.numpy as jnp
from jax import lax
from jax.experimental import pallas as pl
from jax.experimental.pallas import tpu as pltpu
from jax.sharding import PartitionSpec as P


TAYLOR = 4
BUF = 4

time_step = 0.4
half_step = 0.2
xc_factor = 0.9847450218426965


def neighbour_pair(value, axis):
    devices = lax.axis_size(axis)
    up = [(i, i + 1) for i in range(devices - 1)]
    down = [(i + 1, i) for i in range(devices - 1)]
    return lax.ppermute(value, axis, up), lax.ppermute(value, axis, down)


def rounded(value):
    return value.astype(jnp.bfloat16).astype(jnp.float32)


def spread_column(row):
    return jnp.broadcast_to(row, (row.shape[-1], row.shape[-1])).T


def laplace(ref, part, plane):
    center = ref[part, plane]
    side = center.shape[1]
    zero = jnp.zeros((1,) + center.shape[1:], jnp.float32)
    total = ref[part, plane - 1] + ref[part, plane + 1]
    total = total + jnp.concatenate([center[1:], zero]) + jnp.concatenate([zero, center[:-1]])
    level = lax.broadcasted_iota(jnp.int32, center.shape, 1)
    total = total + jnp.where(level == side - 1, 0.0, pltpu.roll(center, side - 1, 1))
    total = total + jnp.where(level == 0, 0.0, pltpu.roll(center, 1, 1))
    return total - 6.0 * center


def kinetic(edge, running, even, odd, slab, grid, exact):
    planes = 3 * slab
    cells = grid[0] * grid[1]
    now, after = even, odd
    for order in range(1, TAYLOR + 1):
        factor = time_step / (2.0 * order)
        spans = ((order, slab, 0), (slab, 2 * slab, None), (2 * slab, planes - order, 1))
        for begin, end, side in spans:
            keep = factor if side is None else edge[side] * factor

            def one(plane, carry, now=now, after=after, keep=keep, side=side, order=order):
                real = -keep * laplace(now, 1, plane)
                imag = keep * laplace(now, 0, plane)
                for part, update in enumerate((real, imag)):
                    if side is None:
                        running[part, plane - slab] = running[part, plane - slab] + update
                    if order < TAYLOR:
                        if not exact:
                            flat = update.reshape(cells, update.shape[-1])
                            update = rounded(flat).reshape(update.shape)
                        after[part, plane] = update
                return carry

            if begin < end:
                lax.fori_loop(begin, end, one, 0)
        now, after = after, now


def fill_phase(potential, row, place, cos_ref, sin_ref, slab):
    cosv = jnp.cos(half_step * potential)
    sinv = jnp.sin(half_step * potential)
    for plane in range(slab):
        cos_ref[place + plane] = spread_column(cosv[row + plane : row + plane + 1])
        sin_ref[place + plane] = spread_column(sinv[row + plane : row + plane + 1])


def start_kernel(slab, grid, scale, edge, low_ref, own_ref, high_ref, field_ref, pot,
                 partial_ref, moved_ref, adjoint_ref, cos_ref, sin_ref,
                 even, odd, running, part_ref, right):
    cells = grid[0] * grid[1]
    half = slab * cells
    lanes = own_ref.shape[-1]
    tail = 2 * half
    box = grid + (lanes,)
    for group, ref in ((0, low_ref), (2, high_ref)):
        extra = ref[tail : tail + 32].astype(jnp.float32)
        whole = extra[0:8] + extra[8:16] + extra[16:24]
        fill_phase(whole, 0, group * slab, cos_ref, sin_ref, slab)
    fill_phase(pot[...], 0, slab, cos_ref, sin_ref, slab)

    for part in range(2):
        for group, ref in enumerate((low_ref, own_ref, high_ref)):

            def begin(plane, carry, ref=ref, group=group, part=part):
                rows = pl.multiple_of((part * slab + plane) * cells, cells)
                value = ref[pl.ds(rows, cells), :].astype(jnp.float32)
                at = group * slab + plane
                real = (cos_ref[at] * value).reshape(box)
                imag = (-sin_ref[at] * value).reshape(box)
                even[0, at] = real
                even[1, at] = imag
                if group == 1:
                    running[0, plane] = real
                    running[1, plane] = imag
                return carry

            lax.fori_loop(0, slab, begin, 0)
        kinetic(edge, running, even, odd, slab, grid, True)
        for plane in range(slab):
            real, imag = turned_back(running, plane, cos_ref, sin_ref, slab)
            low = slice(plane * cells, (plane + 1) * cells)
            high = slice(half + plane * cells, half + (plane + 1) * cells)
            if part == 0:
                part_ref[0, plane] = real
                part_ref[1, plane] = imag
            else:
                kept_real = part_ref[0, plane]
                kept_imag = part_ref[1, plane]
                moved_ref[low] = (kept_real - imag).astype(jnp.bfloat16)
                moved_ref[high] = (kept_imag + real).astype(jnp.bfloat16)
                adjoint_ref[:, low] = (kept_real + imag).T.astype(jnp.bfloat16)
                adjoint_ref[:, high] = (real - kept_imag).T.astype(jnp.bfloat16)
    for place, ref in ((0, field_ref), (2, own_ref)):
        right[:half, place * lanes : (place + 1) * lanes] = ref[:half]
        right[half:, place * lanes : (place + 1) * lanes] = ref[half : 2 * half]
        right[:half, (place + 1) * lanes : (place + 2) * lanes] = ref[half : 2 * half]
        right[half:, (place + 1) * lanes : (place + 2) * lanes] = -ref[:half]
    over = half_dot(adjoint_ref[...], right[...]) * scale
    for index in range(4):
        piece = slice(index * lanes, (index + 1) * lanes)
        partial_ref[piece] = over[:, piece].astype(jnp.bfloat16)


def turned_back(running, plane, cos_ref, sin_ref, slab):
    shape = cos_ref.shape[1:]
    real = running[0, plane].reshape(shape)
    imag = running[1, plane].reshape(shape)
    cosv = cos_ref[slab + plane]
    sinv = sin_ref[slab + plane]
    return cosv * real + sinv * imag, cosv * imag - sinv * real


def first_kernel(slab, grid, scale, edge, low_ref, own_ref, high_ref, adjoint, cos_ref, sin_ref, over,
                 partial_ref, sent_ref, turned_ref, even, odd, running, right):
    cells = grid[0] * grid[1]
    half = slab * cells
    lanes = own_ref.shape[-1]
    box = grid + (lanes,)
    for group, ref in enumerate((low_ref, own_ref, high_ref)):

        def begin(plane, carry, ref=ref, group=group):
            rows = pl.multiple_of(plane * cells, cells)
            real = ref[pl.ds(rows, cells), :].astype(jnp.float32)
            imag = ref[pl.ds(half + rows, cells), :].astype(jnp.float32)
            at = group * slab + plane
            cosv = cos_ref[at]
            sinv = sin_ref[at]
            for part, value in enumerate((cosv * real + sinv * imag, cosv * imag - sinv * real)):
                even[part, at] = rounded(value).reshape(box)
                if group == 1:
                    running[part, plane] = value.reshape(box)
            return carry

        lax.fori_loop(0, slab, begin, 0)
    kinetic(edge, running, even, odd, slab, grid, False)
    for plane in range(slab):
        real, imag = turned_back(running, plane, cos_ref, sin_ref, slab)
        low = slice(plane * cells, (plane + 1) * cells)
        high = slice(half + plane * cells, half + (plane + 1) * cells)
        cosv = cos_ref[slab + plane]
        sinv = sin_ref[slab + plane]
        turned_real = cosv * real + sinv * imag
        turned_imag = cosv * imag - sinv * real
        turned_ref[low] = turned_real
        turned_ref[high] = turned_imag
        sent_ref[low] = turned_real.astype(jnp.bfloat16)
        sent_ref[high] = turned_imag.astype(jnp.bfloat16)
        first_real = real.astype(jnp.bfloat16)
        first_imag = imag.astype(jnp.bfloat16)
        right[low, :lanes] = first_real
        right[low, lanes:] = first_imag
        right[high, :lanes] = first_imag
        right[high, lanes:] = -first_real
    cross = half_dot(adjoint[...], right[...]) * scale
    partial_ref[: 2 * lanes] = over[: 2 * lanes]
    partial_ref[2 * lanes : 3 * lanes] = cross[:, :lanes].astype(jnp.bfloat16)
    partial_ref[3 * lanes : 4 * lanes] = cross[:, lanes:].astype(jnp.bfloat16)
    partial_ref[4 * lanes :] = over[2 * lanes :]


def second_kernel(slab, grid, edge, low, own, high, turned, cos_ref, sin_ref, coupling,
                  occupation, second_ref, coupling_ref, weight_ref,
                  even, odd, running):
    cells = grid[0] * grid[1]
    half = slab * cells
    lanes = own.shape[-1]
    box = grid + (lanes,)
    for part in range(2):
        for group, ref in enumerate((low, own, high)):

            def begin(plane, carry, ref=ref, group=group, part=part):
                at = pl.multiple_of((part * slab + plane) * cells, cells)
                value = ref[pl.ds(at, cells), :].astype(jnp.float32).reshape(box)
                even[part, group * slab + plane] = value
                if group == 1:
                    running[part, plane] = turned[pl.ds(at, cells), :].reshape(box)
                return carry

            lax.fori_loop(0, slab, begin, 0)
    coupling_ref[...] = coupling[...]
    weight_ref[...] = jnp.broadcast_to(occupation[...], weight_ref.shape)
    kinetic(edge, running, even, odd, slab, grid, False)
    for plane in range(slab):
        real, imag = turned_back(running, plane, cos_ref, sin_ref, slab)
        at = plane * cells
        second_ref[at : at + cells] = real
        second_ref[half + at : half + at + cells] = imag


def sum_kernel(parts_ref, out_ref):
    total = parts_ref[0].astype(jnp.float32)
    for index in range(1, parts_ref.shape[0]):
        total = total + parts_ref[index].astype(jnp.float32)
    total = total.astype(jnp.bfloat16)
    for index in range(out_ref.shape[0]):
        out_ref[index] = total


def back_kernel(slab, sums, coupling, moved, start, second, occupation,
                inter_ref, field_ref, density_ref):
    lanes = coupling.shape[-1]
    half = start.shape[0] // 2
    cells = half // slab
    strength = coupling[...]

    def matrix(index):
        return sums[index * lanes : (index + 1) * lanes]

    def mixed(real, imag):
        both = high_dot(strength, jnp.concatenate([real, imag], axis=1)).astype(jnp.bfloat16)
        return both[:, :lanes], both[:, lanes:]

    mix1_real, mix1_imag = mixed(
        matrix(0).astype(jnp.float32), matrix(1).astype(jnp.float32)
    )
    gram_real, gram_imag = matrix(4), matrix(5)
    over_real = matrix(2).astype(jnp.float32) + time_step * (
        half_dot(gram_real, mix1_imag) + half_dot(gram_imag, mix1_real)
    )
    over_imag = matrix(3).astype(jnp.float32) - time_step * (
        half_dot(gram_real, mix1_real) - half_dot(gram_imag, mix1_imag)
    )
    inter_ref[:lanes] = over_real
    inter_ref[lanes:] = over_imag
    mix2_real, mix2_imag = mixed(over_real, over_imag)
    mix1_real_imag = jnp.concatenate([mix1_real, mix1_imag], axis=1)
    mix1_turned = jnp.concatenate([-mix1_imag, mix1_real], axis=1)
    mix2_real_imag = jnp.concatenate([mix2_real, mix2_imag], axis=1)
    mix2_turned = jnp.concatenate([-mix2_imag, mix2_real], axis=1)
    weight = occupation[...]
    for plane in range(slab):
        low = plane * cells
        real_rows = slice(low, low + cells)
        imag_rows = slice(half + low, half + low + cells)
        corr = (
            half_dot(moved[real_rows], mix1_real_imag)
            + half_dot(moved[imag_rows], mix1_turned)
            + half_dot(start[real_rows], mix2_real_imag)
            + half_dot(start[imag_rows], mix2_turned)
        )
        real = second[real_rows] + time_step * corr[:, lanes:]
        imag = second[imag_rows] - time_step * corr[:, :lanes]
        field_ref[real_rows] = real
        field_ref[imag_rows] = imag
        square = real * real + imag * imag
        dense = lax.dot_general(
            weight,
            square,
            (((1,), (1,)), ((), ())),
            precision=lax.Precision.HIGHEST,
            preferred_element_type=jnp.float32,
        )
        for owner in range(density_ref.shape[0]):
            density_ref[owner, plane : plane + 1] = dense[:1]


def tail_kernel(slab, grid, place, gathered, external, field, grid_ref, evolved_ref):
    lanes = external.shape[-1]
    half = field.shape[0] // 2
    cells = half // slab
    side = grid[1]
    own = gathered[place[4]]
    lower = gathered[place[0]]
    upper = gathered[place[1]]
    lower = pltpu.roll(lower, (lanes - place[2] * side) % lanes, 1)
    upper = pltpu.roll(upper, (2 * lanes - BUF * side - place[3] * side) % lanes, 1)
    level = lax.broadcasted_iota(jnp.int32, own.shape, 1) // side
    step = level.astype(jnp.float32)
    weight_low = (step + 1.0) / (BUF + 1.0)
    weight_high = (grid[0] - step) / (BUF + 1.0)
    low = own * weight_low + lower * (1.0 - weight_low)
    high = own * weight_high + upper * (1.0 - weight_high)
    blended = jnp.where(level < BUF, low, jnp.where(level >= grid[0] - BUF, high, own))
    root = jnp.exp(jnp.log(blended + 1e-06) * (1.0 / 3.0))
    new_grid = external[...] - xc_factor * root
    grid_ref[...] = new_grid
    cosv = jnp.cos(half_step * new_grid)
    sinv = jnp.sin(half_step * new_grid)
    for plane in range(slab):
        low_row = plane * cells
        real = field[low_row : low_row + cells]
        imag = field[half + low_row : half + low_row + cells]
        cos_b = spread_column(cosv[plane : plane + 1])
        sin_b = spread_column(sinv[plane : plane + 1])
        evolved_ref[low_row : low_row + cells] = (cos_b * real + sin_b * imag).astype(jnp.bfloat16)
        evolved_ref[half + low_row : half + low_row + cells] = (
            cos_b * imag - sin_b * real
        ).astype(jnp.bfloat16)


def high_dot(left, right):
    return jnp.dot(
        left, right, precision=lax.Precision.HIGHEST, preferred_element_type=jnp.float32
    )


def half_dot(left, right):
    return jnp.dot(left, right, preferred_element_type=jnp.float32)


def pack_kernel(start_ref, pot, out_ref):
    rows = start_ref.shape[0]
    value = pot[...]
    high = rounded(value)
    middle = rounded(value - high)
    low = value - high - middle
    pad = jnp.zeros((8 - value.shape[0], value.shape[1]), value.dtype)
    none = jnp.zeros((8, value.shape[1]), value.dtype)
    out_ref[:rows] = start_ref[...]
    out_ref[rows:] = jnp.concatenate([high, pad, middle, pad, low, pad, none]).astype(jnp.bfloat16)


def scalars(count):
    return [pl.BlockSpec(memory_space=pltpu.SMEM)] + [
        pl.BlockSpec(memory_space=pltpu.VMEM) for _ in range(count)
    ]


def shards(orbitals, initial, potential, external, occupation, coupling, neighbours, offsets):
    slab, rows_y, cols_z, orbits = initial.shape[2:]
    grid = (rows_y, cols_z)
    cells = rows_y * cols_z
    rows = 2 * slab * cells
    start = initial.reshape(rows, orbits)
    devices = lax.axis_size("space")
    place = lax.axis_index("space")
    f32, bf16 = jnp.float32, jnp.bfloat16
    edge = jnp.stack([place > 0, place < devices - 1]).astype(f32)
    planes = (2, 3 * slab) + grid + (orbits,)
    stencil = [pltpu.VMEM(planes, f32), pltpu.VMEM(planes, f32)]
    stencil = stencil + [pltpu.VMEM((2, slab) + grid + (orbits,), f32)]
    shape = jax.ShapeDtypeStruct
    orbs = orbitals.reshape(rows, orbits)
    message = pl.pallas_call(
        pack_kernel,
        out_shape=shape((rows + 32, orbits), bf16),
        compiler_params=pltpu.CompilerParams(vmem_limit_bytes=3 << 20),
        name="pack",
    )(start, potential[0])
    low_m, high_m = neighbour_pair(message, "space")
    low_o, high_o = neighbour_pair(orbs, "space")
    scale = 1.0 / (slab * devices * cells)
    turn = shape((3 * slab, cells, orbits), f32)

    def limit(mib):
        return pltpu.CompilerParams(vmem_limit_bytes=mib << 20)

    over, moved, adjoint, cosv, sinv = pl.pallas_call(
        lambda *refs: start_kernel(slab, grid, scale, *refs),
        out_shape=(
            shape((4 * orbits, orbits), bf16),
            shape((rows, orbits), bf16),
            shape((orbits, rows), bf16),
            turn,
            turn,
        ),
        in_specs=scalars(5),
        scratch_shapes=stencil
        + [
            pltpu.VMEM((2, slab, cells, orbits), f32),
            pltpu.VMEM((rows, 4 * orbits), bf16),
        ],
        compiler_params=limit(16),
        name="start",
    )(edge, low_m, message, high_m, orbs, potential[0])
    partial, sent, turned = pl.pallas_call(
        lambda *refs: first_kernel(slab, grid, scale, *refs),
        out_shape=(
            shape((6 * orbits, orbits), bf16),
            shape((rows, orbits), bf16),
            shape((rows, orbits), f32),
        ),
        in_specs=scalars(7),
        scratch_shapes=stencil + [pltpu.VMEM((rows, 2 * orbits), bf16)],
        compiler_params=limit(14),
        name="first",
    )(edge, low_o, orbs, high_o, adjoint, cosv, sinv, over)
    share = 6 * orbits // devices
    parts = lax.all_to_all(partial.reshape(devices, share, orbits), "space", 0, 0, tiled=True)
    low_s, high_s = neighbour_pair(sent, "space")
    spread = pl.pallas_call(
        sum_kernel,
        out_shape=shape((devices, share, orbits), bf16),
        compiler_params=limit(6),
        name="total",
    )(parts)
    sums = lax.all_to_all(spread, "space", 0, 0, tiled=True)
    sums = sums.reshape(6 * orbits, orbits)
    second, strength, weight = pl.pallas_call(
        lambda *refs: second_kernel(slab, grid, *refs),
        out_shape=(
            shape((rows, orbits), f32),
            shape((orbits, orbits), f32),
            shape((8, orbits), f32),
        ),
        in_specs=scalars(8),
        scratch_shapes=stencil,
        compiler_params=limit(12),
        name="second",
    )(edge, low_s, sent, high_s, turned, cosv, sinv, coupling, occupation.reshape(1, orbits))

    domain_count = neighbours.shape[0]
    intersection, field, density = pl.pallas_call(
        lambda *refs: back_kernel(slab, *refs),
        out_shape=(
            shape((2 * orbits, orbits), f32),
            shape((rows, orbits), f32),
            shape((domain_count, slab, cells), f32),
        ),
        compiler_params=limit(14),
        name="back",
    )(sums, strength, moved, start, second, weight)
    gathered = lax.all_to_all(density, "dom", 0, 0, tiled=True)
    own_index = lax.axis_index("dom")
    mine = lax.dynamic_index_in_dim(neighbours, own_index, 0, keepdims=False)
    shift = lax.dynamic_index_in_dim(offsets, own_index, 0, keepdims=False)
    where = jnp.concatenate([mine, shift, own_index.reshape(1).astype(jnp.int32)])
    new_grid, evolved = pl.pallas_call(
        lambda *refs: tail_kernel(slab, grid, *refs),
        out_shape=(shape((slab, cells), f32), shape((rows, orbits), bf16)),
        in_specs=scalars(3),
        compiler_params=limit(8),
        name="tail",
    )(where, gathered, external[0], field)
    return (
        evolved.reshape(orbitals.shape),
        intersection.reshape(1, 2, orbits, orbits),
        new_grid[None],
    )


def solution(mesh):
    return jax.shard_map(
        shards,
        mesh=mesh,
        in_specs=(
            P("dom", None, "space", None, None, None),
            P("dom", None, "space", None, None, None),
            P("dom", "space", None),
            P("dom", "space", None),
            P(),
            P(),
            P(),
            P(),
        ),
        out_specs=(
            P("dom", None, "space", None, None, None),
            P("dom", None, None, None),
            P("dom", "space", None),
        ),
        check_vma=False,
    )
```

```python
import jax
import jax.numpy as jnp
from jax import lax
from jax.experimental import pallas as pl
from jax.experimental.pallas import tpu as pltpu
from jax.sharding import PartitionSpec as P


TAYLOR = 4
BUF = 4

time_step = 0.4
half_step = 0.2
xc_factor = 0.9847450218426965


def neighbour_pair(value, axis):
    devices = lax.axis_size(axis)
    up = [(i, i + 1) for i in range(devices - 1)]
    down = [(i + 1, i) for i in range(devices - 1)]
    return lax.ppermute(value, axis, up), lax.ppermute(value, axis, down)


def rounded(value):
    return value.astype(jnp.bfloat16).astype(jnp.float32)


def spread_column(row):
    return jnp.broadcast_to(row, (row.shape[-1], row.shape[-1])).T


def laplace(ref, part, plane):
    center = ref[part, plane]
    side = center.shape[1]
    zero = jnp.zeros((1,) + center.shape[1:], jnp.float32)
    total = ref[part, plane - 1] + ref[part, plane + 1]
    total = total + jnp.concatenate([center[1:], zero]) + jnp.concatenate([zero, center[:-1]])
    level = lax.broadcasted_iota(jnp.int32, center.shape, 1)
    total = total + jnp.where(level == side - 1, 0.0, pltpu.roll(center, side - 1, 1))
    total = total + jnp.where(level == 0, 0.0, pltpu.roll(center, 1, 1))
    return total - 6.0 * center


def kinetic(edge, running, even, odd, slab, grid, exact):
    planes = 3 * slab
    cells = grid[0] * grid[1]
    now, after = even, odd
    for order in range(1, TAYLOR + 1):
        factor = time_step / (2.0 * order)
        spans = ((order, slab, 0), (slab, 2 * slab, None), (2 * slab, planes - order, 1))
        for begin, end, side in spans:
            keep = factor if side is None else edge[side] * factor

            def one(plane, carry, now=now, after=after, keep=keep, side=side, order=order):
                real = -keep * laplace(now, 1, plane)
                imag = keep * laplace(now, 0, plane)
                for part, update in enumerate((real, imag)):
                    if side is None:
                        running[part, plane - slab] = running[part, plane - slab] + update
                    if order < TAYLOR:
                        if not exact:
                            flat = update.reshape(cells, update.shape[-1])
                            update = rounded(flat).reshape(update.shape)
                        after[part, plane] = update
                return carry

            if begin < end:
                lax.fori_loop(begin, end, one, 0, unroll=2 if (end - begin) % 2 == 0 else 1)
        now, after = after, now


def fill_phase(potential, row, place, cos_ref, sin_ref, slab):
    cosv = jnp.cos(half_step * potential)
    sinv = jnp.sin(half_step * potential)
    for plane in range(slab):
        cos_ref[place + plane] = spread_column(cosv[row + plane : row + plane + 1])
        sin_ref[place + plane] = spread_column(sinv[row + plane : row + plane + 1])


def start_kernel(slab, grid, scale, edge, low_ref, own_ref, high_ref, field_ref, pot,
                 partial_ref, moved_ref, adjoint_ref, cos_ref, sin_ref,
                 even, odd, running, part_ref, right):
    cells = grid[0] * grid[1]
    half = slab * cells
    lanes = own_ref.shape[-1]
    tail = 2 * half
    box = grid + (lanes,)
    for group, ref in ((0, low_ref), (2, high_ref)):
        extra = ref[tail : tail + 32].astype(jnp.float32)
        whole = extra[0:8] + extra[8:16] + extra[16:24]
        fill_phase(whole, 0, group * slab, cos_ref, sin_ref, slab)
    fill_phase(pot[...], 0, slab, cos_ref, sin_ref, slab)

    for part in range(2):
        for group, ref in enumerate((low_ref, own_ref, high_ref)):

            def begin(plane, carry, ref=ref, group=group, part=part):
                rows = pl.multiple_of((part * slab + plane) * cells, cells)
                value = ref[pl.ds(rows, cells), :].astype(jnp.float32)
                at = group * slab + plane
                real = (cos_ref[at] * value).reshape(box)
                imag = (-sin_ref[at] * value).reshape(box)
                even[0, at] = real
                even[1, at] = imag
                if group == 1:
                    running[0, plane] = real
                    running[1, plane] = imag
                return carry

            lax.fori_loop(0, slab, begin, 0)
        kinetic(edge, running, even, odd, slab, grid, True)
        for plane in range(slab):
            real, imag = turned_back(running, plane, cos_ref, sin_ref, slab)
            low = slice(plane * cells, (plane + 1) * cells)
            high = slice(half + plane * cells, half + (plane + 1) * cells)
            if part == 0:
                part_ref[0, plane] = real
                part_ref[1, plane] = imag
            else:
                kept_real = part_ref[0, plane]
                kept_imag = part_ref[1, plane]
                moved_ref[low] = (kept_real - imag).astype(jnp.bfloat16)
                moved_ref[high] = (kept_imag + real).astype(jnp.bfloat16)
                adjoint_ref[:, low] = (kept_real + imag).T.astype(jnp.bfloat16)
                adjoint_ref[:, high] = (real - kept_imag).T.astype(jnp.bfloat16)
    for place, ref in ((0, field_ref), (2, own_ref)):
        right[:half, place * lanes : (place + 1) * lanes] = ref[:half]
        right[half:, place * lanes : (place + 1) * lanes] = ref[half : 2 * half]
        right[:half, (place + 1) * lanes : (place + 2) * lanes] = ref[half : 2 * half]
        right[half:, (place + 1) * lanes : (place + 2) * lanes] = -ref[:half]
    over = half_dot(adjoint_ref[...], right[...]) * scale
    for index in range(4):
        piece = slice(index * lanes, (index + 1) * lanes)
        partial_ref[piece] = over[:, piece].astype(jnp.bfloat16)


def turned_back(running, plane, cos_ref, sin_ref, slab):
    shape = cos_ref.shape[1:]
    real = running[0, plane].reshape(shape)
    imag = running[1, plane].reshape(shape)
    cosv = cos_ref[slab + plane]
    sinv = sin_ref[slab + plane]
    return cosv * real + sinv * imag, cosv * imag - sinv * real


def first_kernel(slab, grid, scale, edge, low_ref, own_ref, high_ref, adjoint, cos_ref, sin_ref, over,
                 partial_ref, sent_ref, turned_ref, even, odd, running, right):
    cells = grid[0] * grid[1]
    half = slab * cells
    lanes = own_ref.shape[-1]
    box = grid + (lanes,)
    for group, ref in enumerate((low_ref, own_ref, high_ref)):

        def begin(plane, carry, ref=ref, group=group):
            rows = pl.multiple_of(plane * cells, cells)
            real = ref[pl.ds(rows, cells), :].astype(jnp.float32)
            imag = ref[pl.ds(half + rows, cells), :].astype(jnp.float32)
            at = group * slab + plane
            cosv = cos_ref[at]
            sinv = sin_ref[at]
            for part, value in enumerate((cosv * real + sinv * imag, cosv * imag - sinv * real)):
                even[part, at] = rounded(value).reshape(box)
                if group == 1:
                    running[part, plane] = value.reshape(box)
            return carry

        lax.fori_loop(0, slab, begin, 0)
    kinetic(edge, running, even, odd, slab, grid, False)
    for plane in range(slab):
        real, imag = turned_back(running, plane, cos_ref, sin_ref, slab)
        low = slice(plane * cells, (plane + 1) * cells)
        high = slice(half + plane * cells, half + (plane + 1) * cells)
        cosv = cos_ref[slab + plane]
        sinv = sin_ref[slab + plane]
        turned_real = cosv * real + sinv * imag
        turned_imag = cosv * imag - sinv * real
        turned_ref[low] = turned_real
        turned_ref[high] = turned_imag
        sent_ref[low] = turned_real.astype(jnp.bfloat16)
        sent_ref[high] = turned_imag.astype(jnp.bfloat16)
        first_real = real.astype(jnp.bfloat16)
        first_imag = imag.astype(jnp.bfloat16)
        right[low, :lanes] = first_real
        right[low, lanes:] = first_imag
        right[high, :lanes] = first_imag
        right[high, lanes:] = -first_real
    cross = half_dot(adjoint[...], right[...]) * scale
    partial_ref[: 2 * lanes] = over[: 2 * lanes]
    partial_ref[2 * lanes : 3 * lanes] = cross[:, :lanes].astype(jnp.bfloat16)
    partial_ref[3 * lanes : 4 * lanes] = cross[:, lanes:].astype(jnp.bfloat16)
    partial_ref[4 * lanes :] = over[2 * lanes :]


def second_kernel(slab, grid, edge, low, own, high, turned, cos_ref, sin_ref, coupling,
                  occupation, second_ref, coupling_ref, weight_ref,
                  even, odd, running):
    cells = grid[0] * grid[1]
    half = slab * cells
    lanes = own.shape[-1]
    box = grid + (lanes,)
    for part in range(2):
        for group, ref in enumerate((low, own, high)):

            def begin(plane, carry, ref=ref, group=group, part=part):
                at = pl.multiple_of((part * slab + plane) * cells, cells)
                value = ref[pl.ds(at, cells), :].astype(jnp.float32).reshape(box)
                even[part, group * slab + plane] = value
                if group == 1:
                    running[part, plane] = turned[pl.ds(at, cells), :].reshape(box)
                return carry

            lax.fori_loop(0, slab, begin, 0)
    coupling_ref[...] = coupling[...]
    weight_ref[...] = jnp.broadcast_to(occupation[...], weight_ref.shape)
    kinetic(edge, running, even, odd, slab, grid, False)
    for plane in range(slab):
        real, imag = turned_back(running, plane, cos_ref, sin_ref, slab)
        at = plane * cells
        second_ref[at : at + cells] = real
        second_ref[half + at : half + at + cells] = imag


def sum_kernel(parts_ref, out_ref):
    total = parts_ref[0].astype(jnp.float32)
    for index in range(1, parts_ref.shape[0]):
        total = total + parts_ref[index].astype(jnp.float32)
    total = total.astype(jnp.bfloat16)
    for index in range(out_ref.shape[0]):
        out_ref[index] = total


def back_kernel(slab, sums, coupling, moved, start, second, occupation,
                inter_ref, field_ref, density_ref):
    lanes = coupling.shape[-1]
    half = start.shape[0] // 2
    cells = half // slab
    strength = coupling[...]

    def matrix(index):
        return sums[index * lanes : (index + 1) * lanes]

    def mixed(real, imag):
        both = high_dot(strength, jnp.concatenate([real, imag], axis=1)).astype(jnp.bfloat16)
        return both[:, :lanes], both[:, lanes:]

    mix1_real, mix1_imag = mixed(
        matrix(0).astype(jnp.float32), matrix(1).astype(jnp.float32)
    )
    gram_real, gram_imag = matrix(4), matrix(5)
    over_real = matrix(2).astype(jnp.float32) + time_step * (
        half_dot(gram_real, mix1_imag) + half_dot(gram_imag, mix1_real)
    )
    over_imag = matrix(3).astype(jnp.float32) - time_step * (
        half_dot(gram_real, mix1_real) - half_dot(gram_imag, mix1_imag)
    )
    inter_ref[:lanes] = over_real
    inter_ref[lanes:] = over_imag
    mix2_real, mix2_imag = mixed(over_real, over_imag)
    mix1_real_imag = jnp.concatenate([mix1_real, mix1_imag], axis=1)
    mix1_turned = jnp.concatenate([-mix1_imag, mix1_real], axis=1)
    mix2_real_imag = jnp.concatenate([mix2_real, mix2_imag], axis=1)
    mix2_turned = jnp.concatenate([-mix2_imag, mix2_real], axis=1)
    weight = occupation[...]
    for plane in range(slab):
        low = plane * cells
        real_rows = slice(low, low + cells)
        imag_rows = slice(half + low, half + low + cells)
        corr = (
            half_dot(moved[real_rows], mix1_real_imag)
            + half_dot(moved[imag_rows], mix1_turned)
            + half_dot(start[real_rows], mix2_real_imag)
            + half_dot(start[imag_rows], mix2_turned)
        )
        real = second[real_rows] + time_step * corr[:, lanes:]
        imag = second[imag_rows] - time_step * corr[:, :lanes]
        field_ref[real_rows] = real
        field_ref[imag_rows] = imag
        square = real * real + imag * imag
        dense = lax.dot_general(
            weight,
            square,
            (((1,), (1,)), ((), ())),
            precision=lax.Precision.HIGHEST,
            preferred_element_type=jnp.float32,
        )
        for owner in range(density_ref.shape[0]):
            density_ref[owner, plane : plane + 1] = dense[:1]


def tail_kernel(slab, grid, place, gathered, external, field, inter, grid_ref, evolved_ref,
                inter_ref):
    inter_ref[...] = inter[...]
    lanes = external.shape[-1]
    half = field.shape[0] // 2
    cells = half // slab
    side = grid[1]
    own = gathered[place[4]]
    lower = gathered[place[0]]
    upper = gathered[place[1]]
    lower = pltpu.roll(lower, (lanes - place[2] * side) % lanes, 1)
    upper = pltpu.roll(upper, (2 * lanes - BUF * side - place[3] * side) % lanes, 1)
    level = lax.broadcasted_iota(jnp.int32, own.shape, 1) // side
    step = level.astype(jnp.float32)
    weight_low = (step + 1.0) / (BUF + 1.0)
    weight_high = (grid[0] - step) / (BUF + 1.0)
    low = own * weight_low + lower * (1.0 - weight_low)
    high = own * weight_high + upper * (1.0 - weight_high)
    blended = jnp.where(level < BUF, low, jnp.where(level >= grid[0] - BUF, high, own))
    root = jnp.exp(jnp.log(blended + 1e-06) * (1.0 / 3.0))
    new_grid = external[...] - xc_factor * root
    grid_ref[...] = new_grid
    cosv = jnp.cos(half_step * new_grid)
    sinv = jnp.sin(half_step * new_grid)
    for plane in range(slab):
        low_row = plane * cells
        real = field[low_row : low_row + cells]
        imag = field[half + low_row : half + low_row + cells]
        cos_b = spread_column(cosv[plane : plane + 1])
        sin_b = spread_column(sinv[plane : plane + 1])
        evolved_ref[low_row : low_row + cells] = (cos_b * real + sin_b * imag).astype(jnp.bfloat16)
        evolved_ref[half + low_row : half + low_row + cells] = (
            cos_b * imag - sin_b * real
        ).astype(jnp.bfloat16)


def high_dot(left, right):
    return jnp.dot(
        left, right, precision=lax.Precision.HIGHEST, preferred_element_type=jnp.float32
    )


def half_dot(left, right):
    return jnp.dot(left, right, preferred_element_type=jnp.float32)


def pack_kernel(start_ref, pot, out_ref):
    rows = start_ref.shape[0]
    value = pot[...]
    high = rounded(value)
    middle = rounded(value - high)
    low = value - high - middle
    pad = jnp.zeros((8 - value.shape[0], value.shape[1]), value.dtype)
    none = jnp.zeros((8, value.shape[1]), value.dtype)
    out_ref[:rows] = start_ref[...]
    out_ref[rows:] = jnp.concatenate([high, pad, middle, pad, low, pad, none]).astype(jnp.bfloat16)


def scalars(count):
    return [pl.BlockSpec(memory_space=pltpu.SMEM)] + [
        pl.BlockSpec(memory_space=pltpu.VMEM) for _ in range(count)
    ]


def shards(orbitals, initial, potential, external, occupation, coupling, neighbours, offsets):
    slab, rows_y, cols_z, orbits = initial.shape[2:]
    grid = (rows_y, cols_z)
    cells = rows_y * cols_z
    rows = 2 * slab * cells
    start = initial.reshape(rows, orbits)
    devices = lax.axis_size("space")
    place = lax.axis_index("space")
    f32, bf16 = jnp.float32, jnp.bfloat16
    edge = jnp.stack([place > 0, place < devices - 1]).astype(f32)
    planes = (2, 3 * slab) + grid + (orbits,)
    stencil = [pltpu.VMEM(planes, f32), pltpu.VMEM(planes, f32)]
    stencil = stencil + [pltpu.VMEM((2, slab) + grid + (orbits,), f32)]
    shape = jax.ShapeDtypeStruct
    orbs = orbitals.reshape(rows, orbits)
    message = pl.pallas_call(
        pack_kernel,
        out_shape=shape((rows + 32, orbits), bf16),
        compiler_params=pltpu.CompilerParams(vmem_limit_bytes=3 << 20),
        name="pack",
    )(start, potential[0])
    low_m, high_m = neighbour_pair(message, "space")
    low_o, high_o = neighbour_pair(orbs, "space")
    scale = 1.0 / (slab * devices * cells)
    turn = shape((3 * slab, cells, orbits), f32)

    def limit(mib):
        return pltpu.CompilerParams(vmem_limit_bytes=mib << 20)

    over, moved, adjoint, cosv, sinv = pl.pallas_call(
        lambda *refs: start_kernel(slab, grid, scale, *refs),
        out_shape=(
            shape((4 * orbits, orbits), bf16),
            shape((rows, orbits), bf16),
            shape((orbits, rows), bf16),
            turn,
            turn,
        ),
        in_specs=scalars(5),
        scratch_shapes=stencil
        + [
            pltpu.VMEM((2, slab, cells, orbits), f32),
            pltpu.VMEM((rows, 4 * orbits), bf16),
        ],
        compiler_params=limit(16),
        name="start",
    )(edge, low_m, message, high_m, orbs, potential[0])
    partial, sent, turned = pl.pallas_call(
        lambda *refs: first_kernel(slab, grid, scale, *refs),
        out_shape=(
            shape((6 * orbits, orbits), bf16),
            shape((rows, orbits), bf16),
            shape((rows, orbits), f32),
        ),
        in_specs=scalars(7),
        scratch_shapes=stencil + [pltpu.VMEM((rows, 2 * orbits), bf16)],
        compiler_params=limit(14),
        name="first",
    )(edge, low_o, orbs, high_o, adjoint, cosv, sinv, over)
    share = 6 * orbits // devices
    parts = lax.all_to_all(partial.reshape(devices, share, orbits), "space", 0, 0, tiled=True)
    low_s, high_s = neighbour_pair(sent, "space")
    spread = pl.pallas_call(
        sum_kernel,
        out_shape=shape((devices, share, orbits), bf16),
        compiler_params=limit(6),
        name="total",
    )(parts)
    sums = lax.all_to_all(spread, "space", 0, 0, tiled=True)
    sums = sums.reshape(6 * orbits, orbits)
    second, strength, weight = pl.pallas_call(
        lambda *refs: second_kernel(slab, grid, *refs),
        out_shape=(
            shape((rows, orbits), f32),
            shape((orbits, orbits), f32),
            shape((8, orbits), f32),
        ),
        in_specs=scalars(8),
        scratch_shapes=stencil,
        compiler_params=limit(12),
        name="second",
    )(edge, low_s, sent, high_s, turned, cosv, sinv, coupling, occupation.reshape(1, orbits))

    domain_count = neighbours.shape[0]
    intersection, field, density = pl.pallas_call(
        lambda *refs: back_kernel(slab, *refs),
        out_shape=(
            shape((2 * orbits, orbits), f32),
            shape((rows, orbits), f32),
            shape((domain_count, slab, cells), f32),
        ),
        compiler_params=limit(14),
        name="back",
    )(sums, strength, moved, start, second, weight)
    gathered = lax.all_to_all(density, "dom", 0, 0, tiled=True)
    own_index = lax.axis_index("dom")
    mine = lax.dynamic_index_in_dim(neighbours, own_index, 0, keepdims=False)
    shift = lax.dynamic_index_in_dim(offsets, own_index, 0, keepdims=False)
    where = jnp.concatenate([mine, shift, own_index.reshape(1).astype(jnp.int32)])
    new_grid, evolved, intersection = pl.pallas_call(
        lambda *refs: tail_kernel(slab, grid, *refs),
        out_shape=(
            shape((slab, cells), f32),
            shape((rows, orbits), bf16),
            shape((2 * orbits, orbits), f32),
        ),
        in_specs=scalars(4),
        compiler_params=limit(8),
        name="tail",
    )(where, gathered, external[0], field, intersection)
    return (
        evolved.reshape(orbitals.shape),
        intersection.reshape(1, 2, orbits, orbits),
        new_grid[None],
    )


def solution(mesh):
    return jax.shard_map(
        shards,
        mesh=mesh,
        in_specs=(
            P("dom", None, "space", None, None, None),
            P("dom", None, "space", None, None, None),
            P("dom", "space", None),
            P("dom", "space", None),
            P(),
            P(),
            P(),
            P(),
        ),
        out_specs=(
            P("dom", None, "space", None, None, None),
            P("dom", None, None, None),
            P("dom", "space", None),
        ),
        check_vma=False,
    )
```
